32 devices in a mesh: gx: 4 (over z), gy: 8 (over y, x, core).
Axes of the slice: x: 2, y: 2, z: 4, core: 2. Of those that a mesh axis runs over, the one named last changes fastest.
Arguments:
- blocks: bfloat16 [256, 8, 256, 256], P(('gx', 'gy')), may hold values from -0.1875 to 0.1875
- block_cols: int32 [256, 8], P(('gx', 'gy')), may hold values from 0 to 23, as said below
- live_blocks: int32 [256], P(('gx', 'gy')), may hold values from 1 to 8
- send_rows: int32 [32, 4, 4], P(('gx', 'gy')), may hold values from 0 to 7, as said below
- start: float32 [256, 64, 256], P(('gx', 'gy')), may hold values from -6 to 6
- sketch: float32 [64, 256, 256], P(None, ('gx', 'gy')), may hold values from -0.0029296875 to 0.0029296875
Outputs:
- basis: float32 [4, 256, 64, 256], P(None, ('gx', 'gy'))
- factor: float32 [4, 4, 64], replicated
The draws below stay inside these ranges and needn't reach their ends.
Inputs may be any that keep to these rules, and one draw needn't show every extreme that they name: block_cols[i, 0] is block row i itself (i % 8 in the owner's numbering); only the first live_blocks[i] entries of a row are used. `send_rows`: the 4 entries of one device and direction are distinct.
All inputs are finite; a program needn't handle non-finite values.
Results may differ from the reference program's by a relative error of at most 0.0036.
Values may be sent and summed in bfloat16 or wider, within the bound.
A program may use at most 64 MiB of HBM per device.

```python
import jax
import jax.numpy as jnp
from jax import lax

BS = 256
RB = 8
KB = 8
NRHS = 64
SK = 64
STEPS = 3
H = 4
NBR = 256
NROWS = 65536
N_GX = 4
N_GY = 8
DEVICES = 32


def draw_block_cols(key, part):
    own_rows = (jnp.arange(NBR, dtype=jnp.int32) % RB)[:, None]
    others = jax.random.randint(jax.random.fold_in(key, 11), (NBR, KB - 1), 0, RB + 4 * H, dtype=jnp.int32)
    return jnp.concatenate([own_rows, others], axis=1).astype(jnp.int32)


def draw_send_rows(key, part):
    keys = jax.random.split(jax.random.fold_in(key, 7), DEVICES * 4)
    orders = jax.vmap(lambda single: jax.random.permutation(single, RB))(keys)
    return orders[:, :H].reshape(DEVICES, 4, H).astype(jnp.int32)


def plant(array, own_key, low, top_value):
    extent = array.shape
    place = [jax.random.randint(jax.random.fold_in(own_key, axis), (), 0, extent[axis]) for axis in range(len(extent))]
    array = array.at[tuple(place)].set(low)
    longest = extent.index(max(extent))
    place[longest] = (place[longest] + 1) % extent[longest]
    return array.at[tuple(place)].set(top_value)


def steps_of(stream_key, extent, cuts, low, largest):
    def one(position, blocks):
        steps = jax.random.uniform(jax.random.fold_in(jax.random.fold_in(stream_key, 6), position), (blocks,), jnp.float32, low / len(cuts), largest / len(cuts))
        return jnp.repeat(jnp.exp(steps), extent[position] // blocks).reshape((-1,) + (1,) * (len(extent) - position - 1))

    factor_of = one(*cuts[0])
    for cut in cuts[1:]:
        factor_of = factor_of * one(*cut)
    return factor_of


def scatter_about(rng, extent, width, most, cuts=(), kind=jnp.bfloat16):
    entries = width * jax.random.normal(rng, extent, jnp.float32)
    if cuts:
        entries = entries * steps_of(rng, extent, cuts, -0.22, 0.18)
    return jnp.clip(entries, -most, most).astype(kind)


def setup_inputs(seed: int = 0) -> dict:
    key_list = jax.random.split(jax.random.key(seed), 7)
    return {
        "blocks": scatter_about(key_list[0], (NBR, KB, BS, BS), (BS * KB // 2) ** -0.5, 0.1875, ((0, 32),)),
        "block_cols": draw_block_cols(jax.random.fold_in(key_list[6], 71), 0),
        "live_blocks": plant(jax.random.randint(key_list[2], (NBR,), 1, KB + 1), jax.random.fold_in(key_list[2], 1), 1, KB).astype(jnp.int32),
        "send_rows": draw_send_rows(jax.random.fold_in(key_list[6], 71), 0),
        "start": scatter_about(key_list[4], (NBR, NRHS, BS), 1.0, 6.0, ((0, 32),), jnp.float32),
        "sketch": scatter_about(key_list[5], (SK, NBR, BS), (SK * NROWS) ** -0.5, 0.0029296875, ((1, 32),), jnp.float32),
    }


def global_columns(block_cols, send_rows):
    owner = (jnp.arange(NBR, dtype=jnp.int32) // RB)[:, None]
    outer = owner // N_GY
    inner = owner % N_GY
    ghost = block_cols - RB
    direct = jnp.clip(ghost // H, 0, 3).astype(jnp.int32)
    within = (ghost % H).astype(jnp.int32)
    step_gy = jnp.where(direct == 0, -1, jnp.where(direct == 1, 1, 0))
    step_gx = jnp.where(direct == 2, -1, jnp.where(direct == 3, 1, 0))
    source = ((outer + step_gx) % N_GX * N_GY + (inner + step_gy) % N_GY).astype(jnp.int32)
    remote = source * RB + send_rows[source, direct, within]
    return jnp.where(block_cols < RB, owner * RB + block_cols, remote).astype(jnp.int32)

def power_step(vectors, columns, weights, blocks):
    rounded = vectors.astype(jnp.bfloat16)

    def one_device(pieces):
        cols, weight, block = pieces
        picked = rounded[cols].astype(jnp.float32) * weight[:, :, None, None]
        return jnp.einsum('ikrb,ikbc->irc', picked, block.astype(jnp.float32))
    result = lax.map(one_device, (columns.reshape(DEVICES, RB, KB), weights.reshape(DEVICES, RB, KB), blocks.reshape(DEVICES, RB, KB, BS, BS)))
    return result.reshape(NBR, NRHS, BS)

def orthogonalize(sketched):
    count = sketched.shape[0]
    columns = []
    factor = jnp.zeros((count, count, sketched.shape[2]), jnp.float32)
    for column in range(count):
        residue = sketched[column]
        for earlier in range(column):
            coefficient = lax.optimization_barrier(jnp.sum(columns[earlier] * sketched[column], axis=0))
            factor = factor.at[earlier, column].set(coefficient)
            residue = residue - coefficient[None, :] * columns[earlier]
        length = jnp.sqrt(lax.optimization_barrier(jnp.sum(residue * residue, axis=0)) + 1e-06)
        factor = factor.at[column, column].set(length)
        columns.append(residue / length[None, :])
    return factor

def reference(blocks, block_cols, live_blocks, send_rows, start, sketch):
    columns = global_columns(block_cols, send_rows)
    weights = (jnp.arange(KB, dtype=jnp.int32)[None, :] < live_blocks[:, None]).astype(jnp.float32)
    vectors = [start]
    for section in range(STEPS):
        vectors.append(power_step(vectors[-1], columns, weights, blocks))
    sketched = jnp.stack([jnp.einsum('sib,irb->sr', sketch, vector, precision=lax.Precision.HIGHEST) for vector in vectors])
    factor = orthogonalize(sketched)
    result = []
    for column in range(STEPS + 1):
        accum = vectors[column]
        for earlier in range(column):
            accum = accum - factor[earlier, column][None, :, None] * result[earlier]
        result.append(accum / factor[column, column][None, :, None])
    return (jnp.stack(result), factor)
```

```python
import functools

import jax
import jax.numpy as jnp
from jax import lax
from jax.experimental import pallas as pl
from jax.experimental.pallas import tpu as pltpu
from jax.sharding import PartitionSpec as P

STEPS = 3
CHUNKS = 2
MESH = pl.DeviceIdType.MESH
F32 = jnp.float32
BF16 = jnp.bfloat16


def contract_last(a, b):
    return lax.dot_general(a, b, (((1,), (1,)), ((), ())), preferred_element_type=F32)


def split_bf16(x):
    high = x.astype(BF16)
    low = (x - high.astype(F32)).astype(BF16)
    return high, low


def combine(vectors, results, facs, first, past, begin, end, start=None):
    count, rows, rhs, width = vectors.shape
    group = 8
    base = count - results.shape[0]

    def body(n, carry):
        at = pl.ds(pl.multiple_of(n * group, group), group)
        f = facs[at, :]

        def spread(column):
            return jnp.broadcast_to(column, (group, width))

        upper = {
            (m, s): spread(f[:, m * count + s : m * count + s + 1])
            for s in range(first, past)
            for m in range(s)
        }
        inverse = {
            s: spread(1.0 / f[:, s * count + s : s * count + s + 1])
            for s in range(first, past)
        }
        for i in range(rows):
            done = [vectors[m, i, at, :] for m in range(first)]
            for s in range(first, past):
                if s == 0:
                    value = start[i, pl.ds(pl.multiple_of(n * group - begin, group), group), :]
                else:
                    value = vectors[s, i, at, :]
                for m in range(s):
                    value = value - upper[m, s] * done[m]
                value = value * inverse[s]
                done.append(value)
                results[s - base, i, at, :] = value
        return carry

    lax.fori_loop(begin // group, end // group, body, 0)


def power_kernel(
    ngx,
    ngy,
    cols_hbm,
    live_hbm,
    lists_hbm,
    blocks_hbm,
    start_hbm,
    sketch_hbm,
    basis,
    facs,
    cols,
    live,
    lists,
    blk,
    sk,
    shl,
    outgoing,
    kept,
    wsend,
    wrecv,
    gxbuf,
    qbuf,
    qfull,
    plane,
    total3,
    sem_lists,
    sem_local,
    sem_blk,
    halo_s,
    halo_r,
    p1s,
    p1r,
    p2s,
    p2r,
    p3s,
    p3r,
    t1s,
    t1r,
    t2s,
    t2r,
    *halves,
):
    ext = [halves[s * CHUNKS : (s + 1) * CHUNKS] for s in range(STEPS)]
    first = halves[STEPS * CHUNKS : (STEPS + 1) * CHUNKS]
    own = halves[(STEPS + 1) * CHUNKS :]
    count, rows, rhs, width = basis.shape
    part = rhs // CHUNKS
    slots = cols.shape[1]
    send_count = lists.shape[1]
    sk_rows = shl.shape[1] // 2
    lanes = 2 * sk_rows
    zero_slot = halves[0].shape[0] - 1
    chunk = rhs // ngy
    g, h = lax.axis_index("gx"), lax.axis_index("gy")

    def start_copy(c):
        rows_c = pl.ds(c * part, part)
        return pltpu.make_async_copy(
            start_hbm.at[:, rows_c], first[c], sem_local.at[c]
        )

    for c in range(CHUNKS):
        start_copy(c).start()
    scalar_loads = [
        pltpu.make_async_copy(source, target, sem_lists.at[n])
        for n, (source, target) in enumerate(
            ((lists_hbm, lists), (cols_hbm, cols), (live_hbm, live))
        )
    ]
    for load in scalar_loads:
        load.start()
    barrier = pltpu.get_barrier_semaphore()
    for delta in range(1, ngx):
        pl.semaphore_signal(
            barrier, inc=1, device_id={"gx": lax.rem(g + delta, ngx)}, device_id_type=MESH
        )
    for delta in range(1, ngy):
        pl.semaphore_signal(
            barrier, inc=1, device_id={"gy": lax.rem(h + delta, ngy)}, device_id_type=MESH
        )

    parts_wide = sk.shape[0]

    def sketch_copy(c):
        return pltpu.make_async_copy(
            sketch_hbm.at[:, pl.ds(c * 128, 128)], sk.at[c], sem_local.at[CHUNKS + c]
        )

    def block_copy(i):
        return pltpu.make_async_copy(blocks_hbm.at[i], blk.at[i], sem_blk.at[i])

    for half in halves[: STEPS * CHUNKS]:
        half[zero_slot] = jnp.zeros((part, width), BF16)

    targets = (
        {"gy": lax.rem(h + 1, ngy)},
        {"gy": lax.rem(h + ngy - 1, ngy)},
        {"gx": lax.rem(g + 1, ngx)},
        {"gx": lax.rem(g + ngx - 1, ngx)},
    )
    order = (2, 3, 0, 1)

    def halo_copy(s, c, d):
        return pltpu.make_async_remote_copy(
            src_ref=outgoing.at[s, c, d],
            dst_ref=ext[s][c].at[pl.ds(rows + d * send_count, send_count)],
            send_sem=halo_s.at[s, c, d],
            recv_sem=halo_r.at[s, c, d],
            device_id=targets[d],
            device_id_type=MESH,
        )

    def span(c):
        return slice(c * part, (c + 1) * part)

    def gather_outgoing(s, c, d):
        for j in range(send_count):
            outgoing[s, c, d, j] = own[c][lists[d, j]]

    def p1_copy(group, delta):
        to = lax.rem(h + delta, ngy)
        return pltpu.make_async_remote_copy(
            src_ref=wsend.at[group, to],
            dst_ref=wrecv.at[group, delta - 1],
            send_sem=p1s.at[group, delta - 1],
            recv_sem=p1r.at[group, delta - 1],
            device_id={"gy": to},
            device_id_type=MESH,
        )

    def p2_copy(group, delta):
        return pltpu.make_async_remote_copy(
            src_ref=gxbuf.at[group, g],
            dst_ref=gxbuf.at[group, g],
            send_sem=p2s.at[group, delta - 1],
            recv_sem=p2r.at[group, delta - 1],
            device_id={"gx": lax.rem(g + delta, ngx)},
            device_id_type=MESH,
        )

    def p3_copy(delta):
        return pltpu.make_async_remote_copy(
            src_ref=qbuf.at[h],
            dst_ref=qbuf.at[h],
            send_sem=p3s.at[delta - 1],
            recv_sem=p3r.at[delta - 1],
            device_id={"gy": lax.rem(h + delta, ngy)},
            device_id_type=MESH,
        )

    def t1_copy(c, delta):
        return pltpu.make_async_remote_copy(
            src_ref=plane.at[c, h],
            dst_ref=plane.at[c, h],
            send_sem=t1s.at[c, delta - 1],
            recv_sem=t1r.at[c, delta - 1],
            device_id={"gy": lax.rem(h + delta, ngy)},
            device_id_type=MESH,
        )

    def t2_copy(c, delta):
        return pltpu.make_async_remote_copy(
            src_ref=total3.at[c, g],
            dst_ref=total3.at[c, g],
            send_sem=t2s.at[c, delta - 1],
            recv_sem=t2r.at[c, delta - 1],
            device_id={"gx": lax.rem(g + delta, ngx)},
            device_id_type=MESH,
        )

    def low_half(n):
        return lax.broadcasted_iota(jnp.int32, (n, lanes), 1) < sk_rows

    def sketch_of(s, c):
        total = jnp.zeros((2 * part, lanes), F32)
        for i in range(rows):
            high, low = split_bf16(first[c][i] if s == 0 else basis[s, i, span(c), :])
            total = total + contract_last(jnp.concatenate([high, low], axis=0), shl[i])
        total = total[:part] + total[part:]
        return total + pltpu.roll(total, sk_rows, 1)

    def send_group(group, c, both):
        for k in range(part // chunk):
            wsend[group, c * (part // chunk) + k] = both[k * chunk : (k + 1) * chunk]
        if c == CHUNKS - 1:
            for delta in range(1, ngy):
                p1_copy(group, delta).start()

    def after_step(s, c):
        both = sketch_of(s, c)
        if s == 0:
            kept[span(c), :] = both
        elif s == 1:
            send_group(0, c, jnp.where(low_half(part), kept[span(c), :], both))
        elif s == 2:
            send_group(1, c, both)
        else:
            half = part // 2
            plane[c, h] = jnp.where(low_half(half), both[:half], both[half:])
            for delta in range(1, ngy):
                t1_copy(c, delta).start()

    def finish_gy(group):
        total = wsend[group, h]
        for delta in range(1, ngy):
            p1_copy(group, delta).wait_recv()
            total = total + wrecv[group, delta - 1]
        gxbuf[group, g] = total
        for delta in range(1, ngx):
            p2_copy(group, delta).start()

    units = []
    state = {"fac": jnp.zeros((chunk, lanes), F32)}
    lane = lax.broadcasted_iota(jnp.int32, (chunk, lanes), 1)

    def orthogonal(w, earlier):
        residue = w
        found = []
        for unit in earlier:
            coefficient = jnp.sum(unit * w, axis=1, keepdims=True)
            found.append(coefficient)
            residue = residue - coefficient * unit
        square = jnp.sum(residue * residue, axis=1, keepdims=True)
        found.append(jnp.sqrt(square + 1e-06))
        return residue, found

    def finish_gx(group):
        for delta in range(1, ngx):
            p2_copy(group, delta).wait_recv()
        total = gxbuf[group, 0]
        for other in range(1, ngx):
            total = total + gxbuf[group, other]
        for s in (2 * group, 2 * group + 1)[: STEPS - 2 * group]:
            w = total[:, (s % 2) * sk_rows : (s % 2 + 1) * sk_rows]
            residue, found = orthogonal(w, units)
            for m, value in enumerate(found):
                state["fac"] = jnp.where(
                    lane == sk_rows + m * count + s, value, state["fac"]
                )
            units.append(residue / found[-1])

    def send_units():
        qbuf[h, 0] = jnp.concatenate([units[0], units[1]], axis=1)
        qbuf[h, 1] = jnp.where(
            lane < sk_rows, jnp.concatenate([units[2], units[2]], axis=1), state["fac"]
        )
        for delta in range(1, ngy):
            p3_copy(delta).start()

    def take_units():
        for delta in range(1, ngy):
            p3_copy(delta).wait_recv()
        for k in range(ngy):
            for n in range(2):
                qfull[n, k * chunk : (k + 1) * chunk, :] = qbuf[k, n]
        facs[...] = pltpu.roll(qfull[1], sk_rows, 1)

    def finish_plane(c):
        for delta in range(1, ngy):
            t1_copy(c, delta).wait_recv()
        total = plane[c, 0]
        for other in range(1, ngy):
            total = total + plane[c, other]
        total3[c, g] = total
        for delta in range(1, ngx):
            t2_copy(c, delta).start()

    def finish_last(c):
        for delta in range(1, ngx):
            t2_copy(c, delta).wait_recv()
        total = total3[c, 0]
        for other in range(1, ngx):
            total = total + total3[c, other]
        w = jnp.concatenate([total[:, :sk_rows], total[:, sk_rows:]], axis=0)
        pair, single = qfull[0, span(c), :], qfull[1, span(c), :]
        _, found = orthogonal(
            w, [pair[:, :sk_rows], pair[:, sk_rows:], single[:, :sk_rows]]
        )
        wide = lax.broadcasted_iota(jnp.int32, (part, lanes), 1)
        f = facs[span(c), :]
        for m, value in enumerate(found):
            f = jnp.where(wide == m * count + STEPS, value, f)
        facs[span(c), :] = f

    for load in scalar_loads:
        load.wait()
    for c in range(CHUNKS):
        start_copy(c).wait()
        for i in range(rows):
            rounded = first[c][i].astype(BF16)
            own[c][i] = rounded
            ext[0][c][i] = rounded
        if c == 0:
            for n in range(parts_wide):
                sketch_copy(n).start()
            for i in range(rows):
                block_copy(i).start()
            for d in order:
                gather_outgoing(0, c, d)
            pl.semaphore_wait(barrier, ngx + ngy - 2)
        for d in order:
            if c > 0:
                gather_outgoing(0, c, d)
            halo_copy(0, c, d).start()
    for n in range(parts_wide):
        sketch_copy(n).wait()
        for i in range(rows):
            high, low = split_bf16(sk[n, pl.ds(i, sk_rows, stride=rows), :])
            shl[i, :, n * 128 : (n + 1) * 128] = jnp.concatenate([high, low], axis=0)
    for c in range(CHUNKS):
        after_step(0, c)

    for s in range(STEPS):
        for c in range(CHUNKS):
            for d in order:
                halo_copy(s, c, d).wait_recv()

            def row(i):
                parts = [ext[s][c][i]]
                for k in range(1, slots):
                    index = jnp.where(k < live[i], cols[i, k], zero_slot)
                    parts.append(ext[s][c][index])
                picked = jnp.concatenate(parts, axis=1)
                for n in range(width // 128):
                    wide = slice(n * 128, (n + 1) * 128)
                    product = jnp.dot(
                        picked, blk[i, :, wide], preferred_element_type=F32
                    )
                    basis[s + 1, i, span(c), wide] = product
                    if s + 1 < STEPS:
                        rounded = product.astype(BF16)
                        own[c][i, :, wide] = rounded
                        ext[s + 1][c][i, :, wide] = rounded

            def several(n, carry):
                if s == 0 and c == 0:
                    for u in range(rows):
                        block_copy(n * rows + u).wait()
                for u in range(rows):
                    row(n * rows + u)
                return carry

            lax.fori_loop(0, 1, several, 0)
            if s + 1 < STEPS:
                for d in order:
                    gather_outgoing(s + 1, c, d)
                    halo_copy(s + 1, c, d).start()
            after_step(s + 1, c)
            if c == 0 and s > 0:
                finish_gy(s - 1)
        if s == 1:
            finish_gx(0)

    for c in range(CHUNKS - 1):
        finish_plane(c)
    finish_gx(1)
    send_units()
    finish_plane(CHUNKS - 1)
    take_units()
    for c in range(CHUNKS):
        combine(basis, basis, facs, 0, STEPS, c * part, (c + 1) * part, first[c])
    for c in range(CHUNKS):
        finish_last(c)

    for s in range(STEPS):
        for c in range(CHUNKS):
            for d in order:
                halo_copy(s, c, d).wait_send()
    for group in range(2):
        for delta in range(1, ngy):
            p1_copy(group, delta).wait_send()
        for delta in range(1, ngx):
            p2_copy(group, delta).wait_send()
    for delta in range(1, ngy):
        p3_copy(delta).wait_send()
    for c in range(CHUNKS):
        for delta in range(1, ngy):
            t1_copy(c, delta).wait_send()
        for delta in range(1, ngx):
            t2_copy(c, delta).wait_send()


def finish_kernel(vectors, facs, basis_hbm, factor_hbm, last, turned, sem, sem_last):
    count, rows, rhs, width = vectors.shape
    pieces = sem_last.shape[0]
    piece = rhs // pieces

    def early_copy(s):
        return pltpu.make_async_copy(vectors.at[s], basis_hbm.at[s], sem.at[s])

    def last_copy(n):
        at = pl.ds(n * piece, piece)
        return pltpu.make_async_copy(
            last.at[0, :, at], basis_hbm.at[STEPS, :, at], sem_last.at[n]
        )

    factor_copy = pltpu.make_async_copy(turned, factor_hbm, sem.at[STEPS])
    for s in range(STEPS):
        early_copy(s).start()
    for n in range(pieces):
        combine(vectors, last, facs, STEPS, STEPS + 1, n * piece, (n + 1) * piece)
        last_copy(n).start()
    lanes = facs[...].T
    for m in range(count):
        turned[m] = lanes[m * count : (m + 1) * count, :]
    factor_copy.start()
    for s in range(STEPS):
        early_copy(s).wait()
    for n in range(pieces):
        last_copy(n).wait()
    factor_copy.wait()


def on_device(ngx, ngy, blocks, block_cols, live_blocks, send_rows, start, sketch):
    rows, slots, width, _ = blocks.shape
    rhs = start.shape[1]
    sk_rows = sketch.shape[0]
    directions, send_count = send_rows.shape[1:]
    chunk = rhs // ngy
    part = rhs // CHUNKS
    lanes = 2 * sk_rows
    count = STEPS + 1
    places = rows + directions * send_count + 1
    hbm = pl.BlockSpec(memory_space=pltpu.HBM)
    vmem = pl.BlockSpec(memory_space=pltpu.VMEM)
    dma = pltpu.SemaphoreType.DMA
    vectors, facs = pl.pallas_call(
        functools.partial(power_kernel, ngx, ngy),
        name="power",
        out_shape=[
            jax.ShapeDtypeStruct((count, rows, rhs, width), F32),
            jax.ShapeDtypeStruct((rhs, lanes), F32),
        ],
        in_specs=[hbm] * 6,
        out_specs=[vmem, vmem],
        scratch_shapes=[
            pltpu.SMEM(block_cols.shape, jnp.int32),
            pltpu.SMEM(live_blocks.shape, jnp.int32),
            pltpu.SMEM(send_rows.shape[1:], jnp.int32),
            pltpu.VMEM((rows, slots * width, width), BF16),
            pltpu.VMEM((width // 128, sk_rows * rows, 128), F32),
            pltpu.VMEM((rows, lanes, width), BF16),
            pltpu.VMEM((STEPS, CHUNKS, directions, send_count, part, width), BF16),
            pltpu.VMEM((rhs, lanes), F32),
            pltpu.VMEM((2, ngy, chunk, lanes), F32),
            pltpu.VMEM((2, ngy - 1, chunk, lanes), F32),
            pltpu.VMEM((2, ngx, chunk, lanes), F32),
            pltpu.VMEM((ngy, 2, chunk, lanes), F32),
            pltpu.VMEM((2, rhs, lanes), F32),
            pltpu.VMEM((CHUNKS, ngy, part // 2, lanes), F32),
            pltpu.VMEM((CHUNKS, ngx, part // 2, lanes), F32),
            dma((3,)),
            dma((CHUNKS + width // 128,)),
            dma((rows,)),
            dma((STEPS, CHUNKS, directions)),
            dma((STEPS, CHUNKS, directions)),
            dma((2, ngy - 1)),
            dma((2, ngy - 1)),
            dma((2, ngx - 1)),
            dma((2, ngx - 1)),
            dma((ngy - 1,)),
            dma((ngy - 1,)),
            dma((CHUNKS, ngy - 1)),
            dma((CHUNKS, ngy - 1)),
            dma((CHUNKS, ngx - 1)),
            dma((CHUNKS, ngx - 1)),
            *[
                pltpu.VMEM((places, part, width), BF16)
                for half in range(STEPS * CHUNKS)
            ],
            *[pltpu.VMEM((rows, part, width), F32) for c in range(CHUNKS)],
            *[pltpu.VMEM((rows, part, width), BF16) for c in range(CHUNKS)],
        ],
        compiler_params=pltpu.CompilerParams(
            collective_id=0, has_side_effects=True, vmem_limit_bytes=40 * 1024 * 1024
        ),
    )(
        *(
            pltpu.with_memory_space_constraint(array, pltpu.HBM)
            for array in (
                block_cols,
                live_blocks,
                send_rows[0],
                blocks.reshape(rows, slots * width, width),
                start,
                sketch.reshape(sk_rows * rows, width),
            )
        )
    )
    basis, factor = pl.pallas_call(
        finish_kernel,
        name="finish",
        out_shape=[
            jax.ShapeDtypeStruct((count, rows, rhs, width), F32),
            jax.ShapeDtypeStruct((count, count, rhs), F32),
        ],
        in_specs=[vmem, vmem],
        out_specs=[hbm, hbm],
        scratch_shapes=[
            pltpu.VMEM((1, rows, rhs, width), F32),
            pltpu.VMEM((count, count, rhs), F32),
            dma((count,)),
            dma((2,)),
        ],
        compiler_params=pltpu.CompilerParams(vmem_limit_bytes=16 * 1024 * 1024),
    )(vectors, facs)
    return basis, factor


def solution(mesh):
    in_specs = (
        P(("gx", "gy"), None, None, None),
        P(("gx", "gy"), None),
        P(("gx", "gy")),
        P(("gx", "gy"), None, None),
        P(("gx", "gy"), None, None),
        P(None, ("gx", "gy"), None),
    )
    out_specs = (P(None, ("gx", "gy"), None, None), P())
    return jax.shard_map(
        functools.partial(on_device, mesh.shape["gx"], mesh.shape["gy"]),
        mesh=mesh,
        in_specs=in_specs,
        out_specs=out_specs,
        check_vma=False,
    )
```

```python
import functools

import jax
import jax.numpy as jnp
from jax import lax
from jax.experimental import pallas as pl
from jax.experimental.pallas import tpu as pltpu
from jax.sharding import PartitionSpec as P

STEPS = 3
CHUNKS = 2
MESH = pl.DeviceIdType.MESH
F32 = jnp.float32
BF16 = jnp.bfloat16


def contract_last(a, b):
    return lax.dot_general(a, b, (((1,), (1,)), ((), ())), preferred_element_type=F32)


def split_bf16(x):
    high = x.astype(BF16)
    low = (x - high.astype(F32)).astype(BF16)
    return high, low


def combine(vectors, results, facs, first, past, begin, end, start=None):
    count, rows, rhs, width = vectors.shape
    group = 8
    base = count - results.shape[0]

    def body(n, carry):
        at = pl.ds(pl.multiple_of(n * group, group), group)
        f = facs[at, :]

        def spread(column):
            return jnp.broadcast_to(column, (group, width))

        upper = {
            (m, s): spread(f[:, m * count + s : m * count + s + 1])
            for s in range(first, past)
            for m in range(s)
        }
        inverse = {
            s: spread(1.0 / f[:, s * count + s : s * count + s + 1])
            for s in range(first, past)
        }
        for i in range(rows):
            done = [vectors[m, i, at, :] for m in range(first)]
            for s in range(first, past):
                if s == 0:
                    value = start[i, pl.ds(pl.multiple_of(n * group - begin, group), group), :]
                else:
                    value = vectors[s, i, at, :]
                for m in range(s):
                    value = value - upper[m, s] * done[m]
                value = value * inverse[s]
                done.append(value)
                results[s - base, i, at, :] = value
        return carry

    lax.fori_loop(begin // group, end // group, body, 0)


def power_kernel(
    ngx,
    ngy,
    cols_hbm,
    live_hbm,
    lists_hbm,
    blocks_hbm,
    start_hbm,
    sketch_hbm,
    basis,
    facs,
    cols,
    live,
    lists,
    blk,
    sk,
    shl,
    outgoing,
    kept,
    wsend,
    wrecv,
    gxbuf,
    qbuf,
    qfull,
    plane,
    summed,
    sem_lists,
    sem_local,
    sem_blk,
    halo_s,
    halo_r,
    p1s,
    p1r,
    p2s,
    p2r,
    p3s,
    p3r,
    t1s,
    t1r,
    t2s,
    t2r,
    *halves,
):
    ext = [halves[s * CHUNKS : (s + 1) * CHUNKS] for s in range(STEPS)]
    first = halves[STEPS * CHUNKS : (STEPS + 1) * CHUNKS]
    own = halves[(STEPS + 1) * CHUNKS :]
    count, rows, rhs, width = basis.shape
    part = rhs // CHUNKS
    slots = cols.shape[1]
    send_count = lists.shape[1]
    sk_rows = shl.shape[1] // 2
    lanes = 2 * sk_rows
    zero_slot = halves[0].shape[0] - 1
    chunk = rhs // ngy
    g, h = lax.axis_index("gx"), lax.axis_index("gy")

    barrier = pltpu.get_barrier_semaphore()
    for delta in range(1, ngx):
        pl.semaphore_signal(
            barrier, inc=1, device_id={"gx": lax.rem(g + delta, ngx)}, device_id_type=MESH
        )
    for delta in range(1, ngy):
        pl.semaphore_signal(
            barrier, inc=1, device_id={"gy": lax.rem(h + delta, ngy)}, device_id_type=MESH
        )

    def start_copy(c):
        rows_c = pl.ds(c * part, part)
        return pltpu.make_async_copy(
            start_hbm.at[:, rows_c], first[c], sem_local.at[c]
        )

    for c in range(CHUNKS):
        start_copy(c).start()
    scalar_loads = [
        pltpu.make_async_copy(source, target, sem_lists.at[n])
        for n, (source, target) in enumerate(
            ((lists_hbm, lists), (cols_hbm, cols), (live_hbm, live))
        )
    ]
    for load in scalar_loads:
        load.start()
    parts_wide = sk.shape[0]

    def sketch_copy(c):
        return pltpu.make_async_copy(
            sketch_hbm.at[:, pl.ds(c * 128, 128)], sk.at[c], sem_local.at[CHUNKS + c]
        )

    def block_copy(i):
        return pltpu.make_async_copy(blocks_hbm.at[i], blk.at[i], sem_blk.at[i])

    for half in halves[: STEPS * CHUNKS]:
        half[zero_slot] = jnp.zeros((part, width), BF16)

    far = jnp.where(g == ngx - 1, 2, 3)
    order = (far, 5 - far, 0, 1)

    def halo_copy(s, c, d):
        if isinstance(d, int) and d < 2:
            target = {"gy": lax.rem(h + (1 if d == 0 else ngy - 1), ngy)}
        else:
            target = {"gx": lax.rem(g + jnp.where(d == 2, 1, ngx - 1), ngx)}
        return pltpu.make_async_remote_copy(
            src_ref=outgoing.at[s, c, d],
            dst_ref=ext[s][c].at[pl.ds(rows + d * send_count, send_count)],
            send_sem=halo_s.at[s, c, d],
            recv_sem=halo_r.at[s, c, d],
            device_id=target,
            device_id_type=MESH,
        )

    def span(c):
        return slice(c * part, (c + 1) * part)

    def gather_outgoing(s, c, d):
        for j in range(send_count):
            outgoing[s, c, d, j] = own[c][lists[d, j]]

    def p1_copy(delta):
        to = lax.rem(h + delta, ngy)
        return pltpu.make_async_remote_copy(
            src_ref=wsend.at[to],
            dst_ref=wrecv.at[delta - 1],
            send_sem=p1s.at[delta - 1],
            recv_sem=p1r.at[delta - 1],
            device_id={"gy": to},
            device_id_type=MESH,
        )

    def p2_copy(delta):
        return pltpu.make_async_remote_copy(
            src_ref=gxbuf.at[g],
            dst_ref=gxbuf.at[g],
            send_sem=p2s.at[delta - 1],
            recv_sem=p2r.at[delta - 1],
            device_id={"gx": lax.rem(g + delta, ngx)},
            device_id_type=MESH,
        )

    def p3_copy(delta):
        return pltpu.make_async_remote_copy(
            src_ref=qbuf.at[h],
            dst_ref=qbuf.at[h],
            send_sem=p3s.at[delta - 1],
            recv_sem=p3r.at[delta - 1],
            device_id={"gy": lax.rem(h + delta, ngy)},
            device_id_type=MESH,
        )

    def t1_copy(n, c, delta):
        return pltpu.make_async_remote_copy(
            src_ref=plane.at[n, c, h],
            dst_ref=plane.at[n, c, h],
            send_sem=t1s.at[n, c, delta - 1],
            recv_sem=t1r.at[n, c, delta - 1],
            device_id={"gy": lax.rem(h + delta, ngy)},
            device_id_type=MESH,
        )

    def t2_copy(n, c, delta):
        return pltpu.make_async_remote_copy(
            src_ref=summed.at[n, c, g],
            dst_ref=summed.at[n, c, g],
            send_sem=t2s.at[n, c, delta - 1],
            recv_sem=t2r.at[n, c, delta - 1],
            device_id={"gx": lax.rem(g + delta, ngx)},
            device_id_type=MESH,
        )

    def low_half(n):
        return lax.broadcasted_iota(jnp.int32, (n, lanes), 1) < sk_rows

    def sketch_of(s, c):
        total = jnp.zeros((2 * part, lanes), F32)
        for i in range(rows):
            high, low = split_bf16(first[c][i] if s == 0 else basis[s, i, span(c), :])
            total = total + contract_last(jnp.concatenate([high, low], axis=0), shl[i])
        total = total[:part] + total[part:]
        return total + pltpu.roll(total, sk_rows, 1)

    def send_group(c, both):
        for k in range(part // chunk):
            wsend[c * (part // chunk) + k] = both[k * chunk : (k + 1) * chunk]
        if c == CHUNKS - 1:
            for delta in range(1, ngy):
                p1_copy(delta).start()

    def after_step(s, c):
        both = sketch_of(s, c)
        if s == 0:
            kept[span(c), :] = both
        elif s == 1:
            send_group(c, jnp.where(low_half(part), kept[span(c), :], both))
        else:
            half = part // 2
            plane[s - 2, c, h] = jnp.where(low_half(half), both[:half], both[half:])
            for delta in range(1, ngy):
                t1_copy(s - 2, c, delta).start()

    def finish_gy():
        total = wsend[h]
        for delta in range(1, ngy):
            p1_copy(delta).wait_recv()
            total = total + wrecv[delta - 1]
        gxbuf[g] = total
        for delta in range(1, ngx):
            p2_copy(delta).start()

    def orthogonal(w, earlier):
        residue = w
        found = []
        for unit in earlier:
            coefficient = jnp.sum(unit * w, axis=1, keepdims=True)
            found.append(coefficient)
            residue = residue - coefficient * unit
        square = jnp.sum(residue * residue, axis=1, keepdims=True)
        found.append(jnp.sqrt(square + 1e-06))
        return residue, found

    def put(f, s, found):
        lane = lax.broadcasted_iota(jnp.int32, f.shape, 1)
        for m, value in enumerate(found):
            f = jnp.where(lane == m * count + s, value, f)
        return f

    def finish_gx():
        for delta in range(1, ngx):
            p2_copy(delta).wait_recv()
        total = gxbuf[0]
        for other in range(1, ngx):
            total = total + gxbuf[other]
        units = []
        f = jnp.zeros((chunk, lanes), F32)
        for s in range(2):
            w = total[:, s * sk_rows : (s + 1) * sk_rows]
            residue, found = orthogonal(w, units)
            f = put(f, s, found)
            units.append(residue / found[-1])
        qbuf[h, 0] = jnp.concatenate(units, axis=1)
        qbuf[h, 1] = f
        for delta in range(1, ngy):
            p3_copy(delta).start()

    def take_units():
        for delta in range(1, ngy):
            p3_copy(delta).wait_recv()
        for k in range(ngy):
            qfull[k * chunk : (k + 1) * chunk, :] = qbuf[k, 0]
            facs[k * chunk : (k + 1) * chunk, :] = qbuf[k, 1]

    def sum_plane(n, c):
        for delta in range(1, ngy):
            t1_copy(n, c, delta).wait_recv()
        total = plane[n, c, 0]
        for other in range(1, ngy):
            total = total + plane[n, c, other]
        summed[n, c, g] = total

    def send_plane(n, c):
        for delta in range(1, ngx):
            t2_copy(n, c, delta).start()

    third = {}

    def finish_late(n, c):
        for delta in range(1, ngx):
            t2_copy(n, c, delta).wait_recv()
        total = summed[n, c, 0]
        for other in range(1, ngx):
            total = total + summed[n, c, other]
        w = jnp.concatenate([total[:, :sk_rows], total[:, sk_rows:]], axis=0)
        pair = qfull[span(c), :]
        earlier = [pair[:, :sk_rows], pair[:, sk_rows:]]
        if n == 1:
            earlier.append(third[c])
        residue, found = orthogonal(w, earlier)
        facs[span(c), :] = put(facs[span(c), :], n + 2, found)
        if n == 0:
            third[c] = residue / found[-1]

    for load in scalar_loads:
        load.wait()
    for c in range(CHUNKS):
        start_copy(c).wait()
        for i in range(rows):
            rounded = first[c][i].astype(BF16)
            own[c][i] = rounded
            ext[0][c][i] = rounded
        if c == 0:
            for n in range(parts_wide):
                sketch_copy(n).start()
            for i in range(rows):
                block_copy(i).start()
            for d in order:
                gather_outgoing(0, c, d)
            pl.semaphore_wait(barrier, ngx + ngy - 2)
        for d in order:
            if c > 0:
                gather_outgoing(0, c, d)
            halo_copy(0, c, d).start()
    for n in range(parts_wide):
        sketch_copy(n).wait()
        for i in range(rows):
            high, low = split_bf16(sk[n, pl.ds(i, sk_rows, stride=rows), :])
            shl[i, :, n * 128 : (n + 1) * 128] = jnp.concatenate([high, low], axis=0)
    for c in range(CHUNKS):
        after_step(0, c)

    for s in range(STEPS):
        for c in range(CHUNKS):
            for d in order:
                halo_copy(s, c, d).wait_recv()
            if s == STEPS - 1 and c == CHUNKS - 1:
                for other in range(CHUNKS):
                    send_plane(0, other)

            def row(i):
                parts = [ext[s][c][i]]
                for k in range(1, slots):
                    index = jnp.where(k < live[i], cols[i, k], zero_slot)
                    parts.append(ext[s][c][index])
                picked = jnp.concatenate(parts, axis=1)
                for n in range(width // 128):
                    wide = slice(n * 128, (n + 1) * 128)
                    product = jnp.dot(
                        picked, blk[i, :, wide], preferred_element_type=F32
                    )
                    basis[s + 1, i, span(c), wide] = product
                    if s + 1 < STEPS:
                        rounded = product.astype(BF16)
                        own[c][i, :, wide] = rounded
                        ext[s + 1][c][i, :, wide] = rounded

            def several(n, carry):
                if s == 0 and c == 0:
                    for u in range(rows):
                        block_copy(n * rows + u).wait()
                for u in range(rows):
                    row(n * rows + u)
                return carry

            lax.fori_loop(0, 1, several, 0)
            if s + 1 < STEPS:
                for d in order:
                    gather_outgoing(s + 1, c, d)
                    halo_copy(s + 1, c, d).start()
            after_step(s + 1, c)
            if c == 0 and s == 1:
                finish_gy()
            if c == 0 and s == 2:
                finish_gx()
                for other in range(CHUNKS):
                    sum_plane(0, other)

    take_units()
    for c in range(CHUNKS):
        sum_plane(1, c)
        send_plane(1, c)
    for c in range(CHUNKS):
        finish_late(0, c)
        combine(basis, basis, facs, 0, STEPS, c * part, (c + 1) * part, first[c])
    for c in range(CHUNKS):
        finish_late(1, c)

    for s in range(STEPS):
        for c in range(CHUNKS):
            for d in order:
                halo_copy(s, c, d).wait_send()
    for delta in range(1, ngy):
        p1_copy(delta).wait_send()
        p3_copy(delta).wait_send()
    for delta in range(1, ngx):
        p2_copy(delta).wait_send()
    for n in range(2):
        for c in range(CHUNKS):
            for delta in range(1, ngy):
                t1_copy(n, c, delta).wait_send()
            for delta in range(1, ngx):
                t2_copy(n, c, delta).wait_send()


def finish_kernel(vectors, facs, basis_hbm, factor_hbm, last, turned, sem, sem_last):
    count, rows, rhs, width = vectors.shape
    pieces = sem_last.shape[0]
    piece = rhs // pieces

    def early_copy(s):
        return pltpu.make_async_copy(vectors.at[s], basis_hbm.at[s], sem.at[s])

    def last_copy(n):
        at = pl.ds(n * piece, piece)
        return pltpu.make_async_copy(
            last.at[0, :, at], basis_hbm.at[STEPS, :, at], sem_last.at[n]
        )

    factor_copy = pltpu.make_async_copy(turned, factor_hbm, sem.at[STEPS])
    for s in range(STEPS):
        early_copy(s).start()
    for n in range(pieces):
        combine(vectors, last, facs, STEPS, STEPS + 1, n * piece, (n + 1) * piece)
        last_copy(n).start()
    lanes = facs[...].T
    for m in range(count):
        turned[m] = lanes[m * count : (m + 1) * count, :]
    factor_copy.start()
    for s in range(STEPS):
        early_copy(s).wait()
    for n in range(pieces):
        last_copy(n).wait()
    factor_copy.wait()


def on_device(ngx, ngy, blocks, block_cols, live_blocks, send_rows, start, sketch):
    rows, slots, width, _ = blocks.shape
    rhs = start.shape[1]
    sk_rows = sketch.shape[0]
    directions, send_count = send_rows.shape[1:]
    chunk = rhs // ngy
    part = rhs // CHUNKS
    lanes = 2 * sk_rows
    count = STEPS + 1
    places = rows + directions * send_count + 1
    hbm = pl.BlockSpec(memory_space=pltpu.HBM)
    vmem = pl.BlockSpec(memory_space=pltpu.VMEM)
    dma = pltpu.SemaphoreType.DMA
    vectors, facs = pl.pallas_call(
        functools.partial(power_kernel, ngx, ngy),
        name="power",
        out_shape=[
            jax.ShapeDtypeStruct((count, rows, rhs, width), F32),
            jax.ShapeDtypeStruct((rhs, lanes), F32),
        ],
        in_specs=[hbm] * 6,
        out_specs=[vmem, vmem],
        scratch_shapes=[
            pltpu.SMEM(block_cols.shape, jnp.int32),
            pltpu.SMEM(live_blocks.shape, jnp.int32),
            pltpu.SMEM(send_rows.shape[1:], jnp.int32),
            pltpu.VMEM((rows, slots * width, width), BF16),
            pltpu.VMEM((width // 128, sk_rows * rows, 128), F32),
            pltpu.VMEM((rows, lanes, width), BF16),
            pltpu.VMEM((STEPS, CHUNKS, directions, send_count, part, width), BF16),
            pltpu.VMEM((rhs, lanes), F32),
            pltpu.VMEM((ngy, chunk, lanes), F32),
            pltpu.VMEM((ngy - 1, chunk, lanes), F32),
            pltpu.VMEM((ngx, chunk, lanes), F32),
            pltpu.VMEM((ngy, 2, chunk, lanes), F32),
            pltpu.VMEM((rhs, lanes), F32),
            pltpu.VMEM((2, CHUNKS, ngy, part // 2, lanes), F32),
            pltpu.VMEM((2, CHUNKS, ngx, part // 2, lanes), F32),
            dma((3,)),
            dma((CHUNKS + width // 128,)),
            dma((rows,)),
            dma((STEPS, CHUNKS, directions)),
            dma((STEPS, CHUNKS, directions)),
            dma((ngy - 1,)),
            dma((ngy - 1,)),
            dma((ngx - 1,)),
            dma((ngx - 1,)),
            dma((ngy - 1,)),
            dma((ngy - 1,)),
            dma((2, CHUNKS, ngy - 1)),
            dma((2, CHUNKS, ngy - 1)),
            dma((2, CHUNKS, ngx - 1)),
            dma((2, CHUNKS, ngx - 1)),
            *[
                pltpu.VMEM((places, part, width), BF16)
                for half in range(STEPS * CHUNKS)
            ],
            *[pltpu.VMEM((rows, part, width), F32) for c in range(CHUNKS)],
            *[pltpu.VMEM((rows, part, width), BF16) for c in range(CHUNKS)],
        ],
        compiler_params=pltpu.CompilerParams(
            collective_id=0, has_side_effects=True, vmem_limit_bytes=40 * 1024 * 1024
        ),
    )(
        *(
            pltpu.with_memory_space_constraint(array, pltpu.HBM)
            for array in (
                block_cols,
                live_blocks,
                send_rows[0],
                blocks.reshape(rows, slots * width, width),
                start,
                sketch.reshape(sk_rows * rows, width),
            )
        )
    )
    basis, factor = pl.pallas_call(
        finish_kernel,
        name="finish",
        out_shape=[
            jax.ShapeDtypeStruct((count, rows, rhs, width), F32),
            jax.ShapeDtypeStruct((count, count, rhs), F32),
        ],
        in_specs=[vmem, vmem],
        out_specs=[hbm, hbm],
        scratch_shapes=[
            pltpu.VMEM((1, rows, rhs, width), F32),
            pltpu.VMEM((count, count, rhs), F32),
            dma((count,)),
            dma((2,)),
        ],
        compiler_params=pltpu.CompilerParams(vmem_limit_bytes=16 * 1024 * 1024),
    )(vectors, facs)
    return basis, factor


def solution(mesh):
    in_specs = (
        P(("gx", "gy"), None, None, None),
        P(("gx", "gy"), None),
        P(("gx", "gy")),
        P(("gx", "gy"), None, None),
        P(("gx", "gy"), None, None),
        P(None, ("gx", "gy"), None),
    )
    out_specs = (P(None, ("gx", "gy"), None, None), P())
    return jax.shard_map(
        functools.partial(on_device, mesh.shape["gx"], mesh.shape["gy"]),
        mesh=mesh,
        in_specs=in_specs,
        out_specs=out_specs,
        check_vma=False,
    )
```

```python
import functools

import jax
import jax.numpy as jnp
from jax import lax
from jax.experimental import pallas as pl
from jax.experimental.pallas import tpu as pltpu
from jax.sharding import PartitionSpec as P

STEPS = 3
CHUNKS = 2
MESH = pl.DeviceIdType.MESH
F32 = jnp.float32
BF16 = jnp.bfloat16


def split_bf16(x):
    high = x.astype(BF16)
    low = (x - high.astype(F32)).astype(BF16)
    return high, low


def combine(vectors, results, facs, first, past, begin, end, start=None):
    count, rows, rhs, width = vectors.shape
    group = 8
    base = count - results.shape[0]

    def body(n, carry):
        at = pl.ds(pl.multiple_of(n * group, group), group)
        f = facs[at, :]

        def spread(column):
            return jnp.broadcast_to(column, (group, width))

        upper = {
            (m, s): spread(f[:, m * count + s : m * count + s + 1])
            for s in range(first, past)
            for m in range(s)
        }
        inverse = {
            s: spread(1.0 / f[:, s * count + s : s * count + s + 1])
            for s in range(first, past)
        }
        for i in range(rows):
            done = [vectors[m, i, at, :] for m in range(first)]
            for s in range(first, past):
                if s == 0:
                    value = start[i, pl.ds(pl.multiple_of(n * group - begin, group), group), :]
                else:
                    value = vectors[s, i, at, :]
                for m in range(s):
                    value = value - upper[m, s] * done[m]
                value = value * inverse[s]
                done.append(value)
                results[s - base, i, at, :] = value
        return carry

    lax.fori_loop(begin // group, end // group, body, 0)


def power_kernel(
    ngx,
    ngy,
    cols_hbm,
    live_hbm,
    lists_hbm,
    blocks_hbm,
    start_hbm,
    sketch_hbm,
    basis,
    facs,
    cols,
    live,
    lists,
    blk,
    sk,
    shl,
    ahead,
    outgoing,
    kept,
    wsend,
    wrecv,
    gxbuf,
    qbuf,
    qfull,
    plane,
    summed,
    sem_lists,
    sem_local,
    sem_blk,
    halo_s,
    halo_r,
    p1s,
    p1r,
    p2s,
    p2r,
    p3s,
    p3r,
    t1s,
    t1r,
    t2s,
    t2r,
    *halves,
):
    ext = [halves[s * CHUNKS : (s + 1) * CHUNKS] for s in range(STEPS)]
    first = halves[STEPS * CHUNKS : (STEPS + 1) * CHUNKS]
    own = halves[(STEPS + 1) * CHUNKS :]
    count, rows, rhs, width = basis.shape
    part = rhs // CHUNKS
    slots = cols.shape[1]
    send_count = lists.shape[1]
    sk_rows = shl.shape[2] // 2
    lanes = 2 * sk_rows
    zero_slot = halves[0].shape[0] - 1
    chunk = rhs // ngy
    g, h = lax.axis_index("gx"), lax.axis_index("gy")

    barrier = pltpu.get_barrier_semaphore()
    for delta in range(1, ngx):
        pl.semaphore_signal(
            barrier, inc=1, device_id={"gx": lax.rem(g + delta, ngx)}, device_id_type=MESH
        )
    for delta in range(1, ngy):
        pl.semaphore_signal(
            barrier, inc=1, device_id={"gy": lax.rem(h + delta, ngy)}, device_id_type=MESH
        )

    def start_copy(c):
        rows_c = pl.ds(c * part, part)
        return pltpu.make_async_copy(
            start_hbm.at[:, rows_c], first[c], sem_local.at[c]
        )

    for c in range(CHUNKS):
        start_copy(c).start()
    scalar_loads = [
        pltpu.make_async_copy(source, target, sem_lists.at[n])
        for n, (source, target) in enumerate(
            ((lists_hbm, lists), (cols_hbm, cols), (live_hbm, live))
        )
    ]
    for load in scalar_loads:
        load.start()
    parts_wide = sk.shape[0]

    def sketch_copy(c):
        return pltpu.make_async_copy(
            sketch_hbm.at[:, pl.ds(c * 128, 128)], sk.at[c], sem_local.at[CHUNKS + c]
        )

    def block_copy(i):
        return pltpu.make_async_copy(blocks_hbm.at[i], blk.at[i], sem_blk.at[i])

    for half in halves[: STEPS * CHUNKS]:
        half[zero_slot] = jnp.zeros((part, width), BF16)

    far = jnp.where(g == ngx - 1, 2, 3)
    order = (far, 5 - far, 0, 1)

    def halo_copy(s, c, d):
        if isinstance(d, int) and d < 2:
            target = {"gy": lax.rem(h + (1 if d == 0 else ngy - 1), ngy)}
        else:
            target = {"gx": lax.rem(g + jnp.where(d == 2, 1, ngx - 1), ngx)}
        return pltpu.make_async_remote_copy(
            src_ref=outgoing.at[s, c, d],
            dst_ref=ext[s][c].at[pl.ds(rows + d * send_count, send_count)],
            send_sem=halo_s.at[s, c, d],
            recv_sem=halo_r.at[s, c, d],
            device_id=target,
            device_id_type=MESH,
        )

    def span(c):
        return slice(c * part, (c + 1) * part)

    def gather_outgoing(s, c, d):
        for j in range(send_count):
            outgoing[s, c, d, j] = own[c][lists[d, j]]

    def p1_copy(delta):
        to = lax.rem(h + delta, ngy)
        return pltpu.make_async_remote_copy(
            src_ref=wsend.at[to],
            dst_ref=wrecv.at[delta - 1],
            send_sem=p1s.at[delta - 1],
            recv_sem=p1r.at[delta - 1],
            device_id={"gy": to},
            device_id_type=MESH,
        )

    def p2_copy(delta):
        return pltpu.make_async_remote_copy(
            src_ref=gxbuf.at[g],
            dst_ref=gxbuf.at[g],
            send_sem=p2s.at[delta - 1],
            recv_sem=p2r.at[delta - 1],
            device_id={"gx": lax.rem(g + delta, ngx)},
            device_id_type=MESH,
        )

    def p3_copy(delta):
        return pltpu.make_async_remote_copy(
            src_ref=qbuf.at[h],
            dst_ref=qbuf.at[h],
            send_sem=p3s.at[delta - 1],
            recv_sem=p3r.at[delta - 1],
            device_id={"gy": lax.rem(h + delta, ngy)},
            device_id_type=MESH,
        )

    def t1_copy(n, c, delta):
        return pltpu.make_async_remote_copy(
            src_ref=plane.at[n, c, h],
            dst_ref=plane.at[n, c, h],
            send_sem=t1s.at[n, c, delta - 1],
            recv_sem=t1r.at[n, c, delta - 1],
            device_id={"gy": lax.rem(h + delta, ngy)},
            device_id_type=MESH,
        )

    def t2_copy(n, c, delta):
        return pltpu.make_async_remote_copy(
            src_ref=summed.at[n, c, g],
            dst_ref=summed.at[n, c, g],
            send_sem=t2s.at[n, c, delta - 1],
            recv_sem=t2r.at[n, c, delta - 1],
            device_id={"gx": lax.rem(g + delta, ngx)},
            device_id_type=MESH,
        )

    def low_half(n):
        return lax.broadcasted_iota(jnp.int32, (n, lanes), 1) < sk_rows

    def sketch_of(s, c):
        total = jnp.zeros((2 * part, lanes), F32)
        for i in range(rows):
            high, low = split_bf16(first[c][i] if s == 0 else basis[s, i, span(c), :])
            total = total + jnp.dot(
                jnp.concatenate([high, low], axis=0),
                shl[i],
                preferred_element_type=F32,
            )
        total = total[:part] + total[part:]
        return total + pltpu.roll(total, sk_rows, 1)

    def send_group(c, both):
        for k in range(part // chunk):
            wsend[c * (part // chunk) + k] = both[k * chunk : (k + 1) * chunk]
        if c == CHUNKS - 1:
            for delta in range(1, ngy):
                p1_copy(delta).start()

    def after_step(s, c):
        both = sketch_of(s, c)
        if s == 0:
            kept[span(c), :] = both
        elif s == 1:
            send_group(c, jnp.where(low_half(part), kept[span(c), :], both))
        else:
            half = part // 2
            plane[s - 2, c, h] = jnp.where(low_half(half), both[:half], both[half:])
            for delta in range(1, ngy):
                t1_copy(s - 2, c, delta).start()

    def finish_gy():
        total = wsend[h]
        for delta in range(1, ngy):
            p1_copy(delta).wait_recv()
            total = total + wrecv[delta - 1]
        gxbuf[g] = total
        for delta in range(1, ngx):
            p2_copy(delta).start()

    def orthogonal(w, earlier):
        residue = w
        found = []
        for unit in earlier:
            coefficient = jnp.sum(unit * w, axis=1, keepdims=True)
            found.append(coefficient)
            residue = residue - coefficient * unit
        square = jnp.sum(residue * residue, axis=1, keepdims=True)
        found.append(jnp.sqrt(square + 1e-06))
        return residue, found

    def put(f, s, found):
        lane = lax.broadcasted_iota(jnp.int32, f.shape, 1)
        for m, value in enumerate(found):
            f = jnp.where(lane == m * count + s, value, f)
        return f

    def finish_gx():
        for delta in range(1, ngx):
            p2_copy(delta).wait_recv()
        total = gxbuf[0]
        for other in range(1, ngx):
            total = total + gxbuf[other]
        units = []
        f = jnp.zeros((chunk, lanes), F32)
        for s in range(2):
            w = total[:, s * sk_rows : (s + 1) * sk_rows]
            residue, found = orthogonal(w, units)
            f = put(f, s, found)
            units.append(residue / found[-1])
        qbuf[h, 0] = jnp.concatenate(units, axis=1)
        qbuf[h, 1] = f
        for delta in range(1, ngy):
            p3_copy(delta).start()

    def take_units():
        for delta in range(1, ngy):
            p3_copy(delta).wait_recv()
        for k in range(ngy):
            qfull[k * chunk : (k + 1) * chunk, :] = qbuf[k, 0]
            facs[k * chunk : (k + 1) * chunk, :] = qbuf[k, 1]

    def sum_plane(n, c):
        for delta in range(1, ngy):
            t1_copy(n, c, delta).wait_recv()
        total = plane[n, c, 0]
        for other in range(1, ngy):
            total = total + plane[n, c, other]
        summed[n, c, g] = total

    def send_plane(n, c):
        for delta in range(1, ngx):
            t2_copy(n, c, delta).start()

    third = {}

    def finish_late(n, c):
        for delta in range(1, ngx):
            t2_copy(n, c, delta).wait_recv()
        total = summed[n, c, 0]
        for other in range(1, ngx):
            total = total + summed[n, c, other]
        w = jnp.concatenate([total[:, :sk_rows], total[:, sk_rows:]], axis=0)
        pair = qfull[span(c), :]
        earlier = [pair[:, :sk_rows], pair[:, sk_rows:]]
        if n == 1:
            earlier.append(third[c])
        residue, found = orthogonal(w, earlier)
        facs[span(c), :] = put(facs[span(c), :], n + 2, found)
        if n == 0:
            third[c] = residue / found[-1]

    for load in scalar_loads:
        load.wait()
    for c in range(CHUNKS):
        start_copy(c).wait()
        for i in range(rows):
            rounded = first[c][i].astype(BF16)
            own[c][i] = rounded
            ext[0][c][i] = rounded
        if c == 0:
            for n in range(parts_wide):
                sketch_copy(n).start()
            for i in range(rows):
                block_copy(i).start()
            for d in order:
                gather_outgoing(0, c, d)
            pl.semaphore_wait(barrier, ngx + ngy - 2)
        for d in order:
            if c > 0:
                gather_outgoing(0, c, d)
            halo_copy(0, c, d).start()
    for n in range(parts_wide):
        sketch_copy(n).wait()
        for i in range(rows):
            piece = sk[n, pl.ds(i, sk_rows, stride=rows), :]
            high, low = split_bf16(jnp.concatenate([piece, piece], axis=0).T)
            shl[i, n * 128 : (n + 1) * 128, :] = jnp.where(low_half(128), high, low)
    for c in range(CHUNKS):
        after_step(0, c)

    for s in range(STEPS):
        for c in range(CHUNKS):
            for i in range(rows):
                if s == 0 and c == 0:
                    block_copy(i).wait()
                ahead[i] = jnp.dot(own[c][i], blk[i, :width], preferred_element_type=F32)
            for d in order:
                halo_copy(s, c, d).wait_recv()

            def row(i):
                parts = []
                for k in range(1, slots):
                    index = jnp.where(k < live[i], cols[i, k], zero_slot)
                    parts.append(ext[s][c][index])
                picked = jnp.concatenate(parts, axis=1)
                for n in range(width // 128):
                    wide = slice(n * 128, (n + 1) * 128)
                    product = jnp.dot(
                        picked, blk[i, width:, wide], preferred_element_type=F32
                    )
                    product = product + ahead[i, :, wide]
                    basis[s + 1, i, span(c), wide] = product
                    if s + 1 < STEPS:
                        rounded = product.astype(BF16)
                        own[c][i, :, wide] = rounded
                        ext[s + 1][c][i, :, wide] = rounded

            def several(n, carry):
                for u in range(rows):
                    row(n * rows + u)
                return carry

            lax.fori_loop(0, 1, several, 0)
            if s + 1 < STEPS:
                for d in order:
                    gather_outgoing(s + 1, c, d)
                    halo_copy(s + 1, c, d).start()
            after_step(s + 1, c)
            if c == 0 and s == 1:
                finish_gy()
            if c == 0 and s == 2:
                finish_gx()
                for other in range(CHUNKS):
                    sum_plane(0, other)

    for c in range(CHUNKS):
        send_plane(0, c)
    take_units()
    for c in range(CHUNKS):
        sum_plane(1, c)
        send_plane(1, c)
    for c in range(CHUNKS):
        finish_late(0, c)
        combine(basis, basis, facs, 0, STEPS, c * part, (c + 1) * part, first[c])
    for s in range(STEPS):
        for c in range(CHUNKS):
            for d in order:
                halo_copy(s, c, d).wait_send()
    for delta in range(1, ngy):
        p1_copy(delta).wait_send()
        p3_copy(delta).wait_send()
        for n in range(2):
            for c in range(CHUNKS):
                t1_copy(n, c, delta).wait_send()
    for delta in range(1, ngx):
        p2_copy(delta).wait_send()
        for c in range(CHUNKS):
            t2_copy(0, c, delta).wait_send()
    for c in range(CHUNKS):
        finish_late(1, c)

    for c in range(CHUNKS):
        for delta in range(1, ngx):
            t2_copy(1, c, delta).wait_send()


def finish_kernel(vectors, facs, basis_hbm, factor_hbm, last, turned, sem, sem_last):
    count, rows, rhs, width = vectors.shape
    pieces = sem_last.shape[0]
    piece = rhs // pieces

    def early_copy(s):
        return pltpu.make_async_copy(vectors.at[s], basis_hbm.at[s], sem.at[s])

    def last_copy(n):
        at = pl.ds(n * piece, piece)
        return pltpu.make_async_copy(
            last.at[0, :, at], basis_hbm.at[STEPS, :, at], sem_last.at[n]
        )

    factor_copy = pltpu.make_async_copy(turned, factor_hbm, sem.at[STEPS])
    for s in range(STEPS):
        early_copy(s).start()
    for n in range(pieces):
        combine(vectors, last, facs, STEPS, STEPS + 1, n * piece, (n + 1) * piece)
        last_copy(n).start()
    lanes = facs[...].T
    for m in range(count):
        turned[m] = lanes[m * count : (m + 1) * count, :]
    factor_copy.start()
    for s in range(STEPS):
        early_copy(s).wait()
    for n in range(pieces):
        last_copy(n).wait()
    factor_copy.wait()


def on_device(ngx, ngy, blocks, block_cols, live_blocks, send_rows, start, sketch):
    rows, slots, width, _ = blocks.shape
    rhs = start.shape[1]
    sk_rows = sketch.shape[0]
    directions, send_count = send_rows.shape[1:]
    chunk = rhs // ngy
    part = rhs // CHUNKS
    lanes = 2 * sk_rows
    count = STEPS + 1
    places = rows + directions * send_count + 1
    hbm = pl.BlockSpec(memory_space=pltpu.HBM)
    vmem = pl.BlockSpec(memory_space=pltpu.VMEM)
    dma = pltpu.SemaphoreType.DMA
    vectors, facs = pl.pallas_call(
        functools.partial(power_kernel, ngx, ngy),
        name="power",
        out_shape=[
            jax.ShapeDtypeStruct((count, rows, rhs, width), F32),
            jax.ShapeDtypeStruct((rhs, lanes), F32),
        ],
        in_specs=[hbm] * 6,
        out_specs=[vmem, vmem],
        scratch_shapes=[
            pltpu.SMEM(block_cols.shape, jnp.int32),
            pltpu.SMEM(live_blocks.shape, jnp.int32),
            pltpu.SMEM(send_rows.shape[1:], jnp.int32),
            pltpu.VMEM((rows, slots * width, width), BF16),
            pltpu.VMEM((width // 128, sk_rows * rows, 128), F32),
            pltpu.VMEM((rows, width, lanes), BF16),
            pltpu.VMEM((rows, part, width), F32),
            pltpu.VMEM((STEPS, CHUNKS, directions, send_count, part, width), BF16),
            pltpu.VMEM((rhs, lanes), F32),
            pltpu.VMEM((ngy, chunk, lanes), F32),
            pltpu.VMEM((ngy - 1, chunk, lanes), F32),
            pltpu.VMEM((ngx, chunk, lanes), F32),
            pltpu.VMEM((ngy, 2, chunk, lanes), F32),
            pltpu.VMEM((rhs, lanes), F32),
            pltpu.VMEM((2, CHUNKS, ngy, part // 2, lanes), F32),
            pltpu.VMEM((2, CHUNKS, ngx, part // 2, lanes), F32),
            dma((3,)),
            dma((CHUNKS + width // 128,)),
            dma((rows,)),
            dma((STEPS, CHUNKS, directions)),
            dma((STEPS, CHUNKS, directions)),
            dma((ngy - 1,)),
            dma((ngy - 1,)),
            dma((ngx - 1,)),
            dma((ngx - 1,)),
            dma((ngy - 1,)),
            dma((ngy - 1,)),
            dma((2, CHUNKS, ngy - 1)),
            dma((2, CHUNKS, ngy - 1)),
            dma((2, CHUNKS, ngx - 1)),
            dma((2, CHUNKS, ngx - 1)),
            *[
                pltpu.VMEM((places, part, width), BF16)
                for half in range(STEPS * CHUNKS)
            ],
            *[pltpu.VMEM((rows, part, width), F32) for c in range(CHUNKS)],
            *[pltpu.VMEM((rows, part, width), BF16) for c in range(CHUNKS)],
        ],
        compiler_params=pltpu.CompilerParams(
            collective_id=0, has_side_effects=True, vmem_limit_bytes=40 * 1024 * 1024
        ),
    )(
        *(
            pltpu.with_memory_space_constraint(array, pltpu.HBM)
            for array in (
                block_cols,
                live_blocks,
                send_rows[0],
                blocks.reshape(rows, slots * width, width),
                start,
                sketch.reshape(sk_rows * rows, width),
            )
        )
    )
    basis, factor = pl.pallas_call(
        finish_kernel,
        name="finish",
        out_shape=[
            jax.ShapeDtypeStruct((count, rows, rhs, width), F32),
            jax.ShapeDtypeStruct((count, count, rhs), F32),
        ],
        in_specs=[vmem, vmem],
        out_specs=[hbm, hbm],
        scratch_shapes=[
            pltpu.VMEM((1, rows, rhs, width), F32),
            pltpu.VMEM((count, count, rhs), F32),
            dma((count,)),
            dma((2,)),
        ],
        compiler_params=pltpu.CompilerParams(vmem_limit_bytes=16 * 1024 * 1024),
    )(vectors, facs)
    return basis, factor


def solution(mesh):
    in_specs = (
        P(("gx", "gy"), None, None, None),
        P(("gx", "gy"), None),
        P(("gx", "gy")),
        P(("gx", "gy"), None, None),
        P(("gx", "gy"), None, None),
        P(None, ("gx", "gy"), None),
    )
    out_specs = (P(None, ("gx", "gy"), None, None), P())
    return jax.shard_map(
        functools.partial(on_device, mesh.shape["gx"], mesh.shape["gy"]),
        mesh=mesh,
        in_specs=in_specs,
        out_specs=out_specs,
        check_vma=False,
    )
```

```python
import functools

import jax
import jax.numpy as jnp
from jax import lax
from jax.experimental import pallas as pl
from jax.experimental.pallas import tpu as pltpu
from jax.sharding import PartitionSpec as P

STEPS = 3
CHUNKS = 2
MESH = pl.DeviceIdType.MESH
F32 = jnp.float32
BF16 = jnp.bfloat16


def split_bf16(x):
    high = x.astype(BF16)
    low = (x - high.astype(F32)).astype(BF16)
    return high, low


def combine(vectors, results, facs, first, past, begin, end, start=None):
    count, rows, rhs, width = vectors.shape
    group = 8
    base = count - results.shape[0]

    def body(n, carry):
        at = pl.ds(pl.multiple_of(n * group, group), group)
        f = facs[at, :]

        def spread(column):
            return jnp.broadcast_to(column, (group, width))

        upper = {
            (m, s): spread(f[:, m * count + s : m * count + s + 1])
            for s in range(first, past)
            for m in range(s)
        }
        inverse = {
            s: spread(1.0 / f[:, s * count + s : s * count + s + 1])
            for s in range(first, past)
        }
        for i in range(rows):
            done = [vectors[m, i, at, :] for m in range(first)]
            for s in range(first, past):
                if s == 0:
                    value = start[i, pl.ds(pl.multiple_of(n * group - begin, group), group), :]
                else:
                    value = vectors[s, i, at, :]
                for m in range(s):
                    value = value - upper[m, s] * done[m]
                value = value * inverse[s]
                done.append(value)
                results[s - base, i, at, :] = value
        return carry

    lax.fori_loop(begin // group, end // group, body, 0)


def power_kernel(
    ngx,
    ngy,
    cols_hbm,
    live_hbm,
    lists_hbm,
    blocks_hbm,
    start_hbm,
    sketch_hbm,
    basis,
    facs,
    cols,
    live,
    lists,
    blk,
    sk,
    shl,
    ahead,
    outgoing,
    kept,
    wsend,
    wrecv,
    gxbuf,
    qbuf,
    qfull,
    plane,
    summed,
    sem_lists,
    sem_local,
    sem_blk,
    halo_s,
    halo_r,
    p1s,
    p1r,
    p2s,
    p2r,
    p3s,
    p3r,
    t1s,
    t1r,
    t2s,
    t2r,
    *halves,
):
    ext = [halves[s * CHUNKS : (s + 1) * CHUNKS] for s in range(STEPS)]
    first = halves[STEPS * CHUNKS : (STEPS + 1) * CHUNKS]
    own = halves[(STEPS + 1) * CHUNKS :]
    count, rows, rhs, width = basis.shape
    part = rhs // CHUNKS
    slots = cols.shape[1]
    send_count = lists.shape[1]
    sk_rows = shl.shape[2] // 2
    lanes = 2 * sk_rows
    zero_slot = halves[0].shape[0] - 1
    chunk = rhs // ngy
    g, h = lax.axis_index("gx"), lax.axis_index("gy")

    barrier = pltpu.get_barrier_semaphore()
    for delta in range(1, ngx):
        pl.semaphore_signal(
            barrier, inc=1, device_id={"gx": lax.rem(g + delta, ngx)}, device_id_type=MESH
        )
    for delta in range(1, ngy):
        pl.semaphore_signal(
            barrier, inc=1, device_id={"gy": lax.rem(h + delta, ngy)}, device_id_type=MESH
        )

    def start_copy(c):
        rows_c = pl.ds(c * part, part)
        return pltpu.make_async_copy(
            start_hbm.at[:, rows_c], first[c], sem_local.at[c]
        )

    for c in range(CHUNKS):
        start_copy(c).start()
    scalar_loads = [
        pltpu.make_async_copy(source, target, sem_lists.at[n])
        for n, (source, target) in enumerate(
            ((lists_hbm, lists), (cols_hbm, cols), (live_hbm, live))
        )
    ]
    for load in scalar_loads:
        load.start()
    parts_wide = sk.shape[0]

    def sketch_copy(c):
        return pltpu.make_async_copy(
            sketch_hbm.at[:, pl.ds(c * 128, 128)], sk.at[c], sem_local.at[CHUNKS + c]
        )

    def block_copy(i):
        return pltpu.make_async_copy(blocks_hbm.at[i], blk.at[i], sem_blk.at[i])

    for half in halves[: STEPS * CHUNKS]:
        half[zero_slot] = jnp.zeros((part, width), BF16)

    far = jnp.where(g == ngx - 1, 2, 3)
    order = (far, 5 - far, 0, 1)

    def halo_copy(s, c, d):
        if isinstance(d, int) and d < 2:
            target = {"gy": lax.rem(h + (1 if d == 0 else ngy - 1), ngy)}
        else:
            target = {"gx": lax.rem(g + jnp.where(d == 2, 1, ngx - 1), ngx)}
        return pltpu.make_async_remote_copy(
            src_ref=outgoing.at[s, c, d],
            dst_ref=ext[s][c].at[pl.ds(rows + d * send_count, send_count)],
            send_sem=halo_s.at[s, c, d],
            recv_sem=halo_r.at[s, c, d],
            device_id=target,
            device_id_type=MESH,
        )

    def span(c):
        return slice(c * part, (c + 1) * part)

    def gather_outgoing(s, c, d):
        for j in range(send_count):
            outgoing[s, c, d, j] = own[c][lists[d, j]]

    def p1_copy(delta):
        to = lax.rem(h + delta, ngy)
        return pltpu.make_async_remote_copy(
            src_ref=wsend.at[to],
            dst_ref=wrecv.at[delta - 1],
            send_sem=p1s.at[delta - 1],
            recv_sem=p1r.at[delta - 1],
            device_id={"gy": to},
            device_id_type=MESH,
        )

    def p2_copy(delta):
        return pltpu.make_async_remote_copy(
            src_ref=gxbuf.at[g],
            dst_ref=gxbuf.at[g],
            send_sem=p2s.at[delta - 1],
            recv_sem=p2r.at[delta - 1],
            device_id={"gx": lax.rem(g + delta, ngx)},
            device_id_type=MESH,
        )

    def p3_copy(delta):
        return pltpu.make_async_remote_copy(
            src_ref=qbuf.at[h],
            dst_ref=qbuf.at[h],
            send_sem=p3s.at[delta - 1],
            recv_sem=p3r.at[delta - 1],
            device_id={"gy": lax.rem(h + delta, ngy)},
            device_id_type=MESH,
        )

    def t1_copy(n, c, delta):
        return pltpu.make_async_remote_copy(
            src_ref=plane.at[n, c, h],
            dst_ref=plane.at[n, c, h],
            send_sem=t1s.at[n, c, delta - 1],
            recv_sem=t1r.at[n, c, delta - 1],
            device_id={"gy": lax.rem(h + delta, ngy)},
            device_id_type=MESH,
        )

    def t2_copy(n, c, delta):
        return pltpu.make_async_remote_copy(
            src_ref=summed.at[n, c, g],
            dst_ref=summed.at[n, c, g],
            send_sem=t2s.at[n, c, delta - 1],
            recv_sem=t2r.at[n, c, delta - 1],
            device_id={"gx": lax.rem(g + delta, ngx)},
            device_id_type=MESH,
        )

    def low_half(n):
        return lax.broadcasted_iota(jnp.int32, (n, lanes), 1) < sk_rows

    def sketch_of(s, c):
        total = jnp.zeros((2 * part, lanes), F32)
        for i in range(rows):
            high, low = split_bf16(first[c][i] if s == 0 else basis[s, i, span(c), :])
            total = total + jnp.dot(
                jnp.concatenate([high, low], axis=0),
                shl[i],
                preferred_element_type=F32,
            )
        total = total[:part] + total[part:]
        return total + pltpu.roll(total, sk_rows, 1)

    def send_group(c, both):
        for k in range(part // chunk):
            wsend[c * (part // chunk) + k] = both[k * chunk : (k + 1) * chunk]
        if c == CHUNKS - 1:
            for delta in range(1, ngy):
                p1_copy(delta).start()

    def after_step(s, c):
        both = sketch_of(s, c)
        if s == 0:
            kept[span(c), :] = both
        elif s == 1:
            send_group(c, jnp.where(low_half(part), kept[span(c), :], both))
        else:
            half = part // 2
            plane[s - 2, c, h] = jnp.where(low_half(half), both[:half], both[half:])
            for delta in range(1, ngy):
                t1_copy(s - 2, c, delta).start()

    def finish_gy():
        total = wsend[h]
        for delta in range(1, ngy):
            p1_copy(delta).wait_recv()
            total = total + wrecv[delta - 1]
        gxbuf[g] = total
        for delta in range(1, ngx):
            p2_copy(delta).start()

    def orthogonal(w, earlier):
        residue = w
        found = []
        for unit in earlier:
            coefficient = jnp.sum(unit * w, axis=1, keepdims=True)
            found.append(coefficient)
            residue = residue - coefficient * unit
        square = jnp.sum(residue * residue, axis=1, keepdims=True)
        found.append(jnp.sqrt(square + 1e-06))
        return residue, found

    def put(f, s, found):
        lane = lax.broadcasted_iota(jnp.int32, f.shape, 1)
        for m, value in enumerate(found):
            f = jnp.where(lane == m * count + s, value, f)
        return f

    def finish_gx():
        for delta in range(1, ngx):
            p2_copy(delta).wait_recv()
        total = gxbuf[0]
        for other in range(1, ngx):
            total = total + gxbuf[other]
        units = []
        f = jnp.zeros((chunk, lanes), F32)
        for s in range(2):
            w = total[:, s * sk_rows : (s + 1) * sk_rows]
            residue, found = orthogonal(w, units)
            f = put(f, s, found)
            units.append(residue / found[-1])
        qbuf[h, 0] = jnp.concatenate(units, axis=1)
        qbuf[h, 1] = f
        for delta in range(1, ngy):
            p3_copy(delta).start()

    def take_units():
        for delta in range(1, ngy):
            p3_copy(delta).wait_recv()
        for k in range(ngy):
            qfull[k * chunk : (k + 1) * chunk, :] = qbuf[k, 0]
            facs[k * chunk : (k + 1) * chunk, :] = qbuf[k, 1]

    def sum_plane(n, c):
        for delta in range(1, ngy):
            t1_copy(n, c, delta).wait_recv()
        total = plane[n, c, 0]
        for other in range(1, ngy):
            total = total + plane[n, c, other]
        summed[n, c, g] = total

    def send_plane(n, c):
        for delta in range(1, ngx):
            t2_copy(n, c, delta).start()

    third = {}

    def finish_late(n, c):
        for delta in range(1, ngx):
            t2_copy(n, c, delta).wait_recv()
        total = summed[n, c, 0]
        for other in range(1, ngx):
            total = total + summed[n, c, other]
        w = jnp.concatenate([total[:, :sk_rows], total[:, sk_rows:]], axis=0)
        pair = qfull[span(c), :]
        earlier = [pair[:, :sk_rows], pair[:, sk_rows:]]
        if n == 1:
            earlier.append(third[c])
        residue, found = orthogonal(w, earlier)
        facs[span(c), :] = put(facs[span(c), :], n + 2, found)
        if n == 0:
            third[c] = residue / found[-1]

    for load in scalar_loads:
        load.wait()
    def prepare_sketch():
        for n in range(parts_wide):
            sketch_copy(n).wait()
            for i in range(rows):
                piece = sk[n, pl.ds(i, sk_rows, stride=rows), :]
                high, low = split_bf16(jnp.concatenate([piece, piece], axis=0).T)
                shl[i, n * 128 : (n + 1) * 128, :] = jnp.where(low_half(128), high, low)

    for c in range(CHUNKS):
        start_copy(c).wait()
        for i in range(rows):
            rounded = first[c][i].astype(BF16)
            own[c][i] = rounded
            ext[0][c][i] = rounded
        if c == 0:
            for n in range(parts_wide):
                sketch_copy(n).start()
            for i in range(rows):
                block_copy(i).start()
        for d in order:
            gather_outgoing(0, c, d)
        if c == 0:
            pl.semaphore_wait(barrier, ngx + ngy - 2)
        if c == 1:
            prepare_sketch()
        for n, d in enumerate(order):
            if c > 0 and n < 2:
                halo_copy(0, c - 1, d).wait_send()
            halo_copy(0, c, d).start()

    for c in range(CHUNKS):
        after_step(0, c)

    for s in range(STEPS):
        for c in range(CHUNKS):
            for i in range(rows):
                if s == 0 and c == 0:
                    block_copy(i).wait()
                ahead[i] = jnp.dot(own[c][i], blk[i, :width], preferred_element_type=F32)
            for d in order:
                halo_copy(s, c, d).wait_recv()

            def row(i):
                parts = []
                for k in range(1, slots):
                    index = jnp.where(k < live[i], cols[i, k], zero_slot)
                    parts.append(ext[s][c][index])
                picked = jnp.concatenate(parts, axis=1)
                for n in range(width // 128):
                    wide = slice(n * 128, (n + 1) * 128)
                    product = jnp.dot(
                        picked, blk[i, width:, wide], preferred_element_type=F32
                    )
                    product = product + ahead[i, :, wide]
                    basis[s + 1, i, span(c), wide] = product
                    if s + 1 < STEPS:
                        rounded = product.astype(BF16)
                        own[c][i, :, wide] = rounded
                        ext[s + 1][c][i, :, wide] = rounded

            def several(n, carry):
                for u in range(rows):
                    row(n * rows + u)
                return carry

            lax.fori_loop(0, 1, several, 0)
            if s + 1 < STEPS:
                for d in order:
                    gather_outgoing(s + 1, c, d)
                    halo_copy(s + 1, c, d).start()
            after_step(s + 1, c)
            if c == 1 and s == 1:
                finish_gy()

    finish_gx()
    for c in range(CHUNKS):
        sum_plane(0, c)
        send_plane(0, c)
    for c in range(CHUNKS):
        sum_plane(1, c)
        send_plane(1, c)
    take_units()
    for c in range(CHUNKS):
        finish_late(0, c)
        combine(basis, basis, facs, 0, STEPS, c * part, (c + 1) * part, first[c])
    for s in range(STEPS):
        for c in range(CHUNKS):
            for n, d in enumerate(order):
                if s > 0 or c == CHUNKS - 1 or n >= 2:
                    halo_copy(s, c, d).wait_send()
    for delta in range(1, ngy):
        p1_copy(delta).wait_send()
        p3_copy(delta).wait_send()
        for n in range(2):
            for c in range(CHUNKS):
                t1_copy(n, c, delta).wait_send()
    for delta in range(1, ngx):
        p2_copy(delta).wait_send()
        for c in range(CHUNKS):
            t2_copy(0, c, delta).wait_send()
    for c in range(CHUNKS):
        finish_late(1, c)
        if c + 1 < CHUNKS:
            combine(
                basis, basis, facs, STEPS, STEPS + 1, c * part, (c + 1) * part
            )

    for c in range(CHUNKS):
        for delta in range(1, ngx):
            t2_copy(1, c, delta).wait_send()


def finish_kernel(vectors, facs, basis_hbm, factor_hbm, last, turned, sem, sem_last):
    count, rows, rhs, width = vectors.shape
    pieces = sem_last.shape[0]
    begin = rhs - rhs // CHUNKS
    piece = (rhs - begin) // pieces

    def early_copy(s):
        at = pl.ds(0, begin if s == STEPS else rhs)
        return pltpu.make_async_copy(
            vectors.at[s, :, at], basis_hbm.at[s, :, at], sem.at[s]
        )

    def last_copy(n):
        at = pl.ds(begin + n * piece, piece)
        return pltpu.make_async_copy(
            last.at[0, :, at], basis_hbm.at[STEPS, :, at], sem_last.at[n]
        )

    factor_copy = pltpu.make_async_copy(turned, factor_hbm, sem.at[count])
    for s in range(count):
        early_copy(s).start()
    for n in range(pieces):
        at = begin + n * piece
        combine(vectors, last, facs, STEPS, STEPS + 1, at, at + piece)
        last_copy(n).start()
    lanes = facs[...].T
    for m in range(count):
        turned[m] = lanes[m * count : (m + 1) * count, :]
    factor_copy.start()
    for s in range(count):
        early_copy(s).wait()
    for n in range(pieces):
        last_copy(n).wait()
    factor_copy.wait()


def on_device(ngx, ngy, blocks, block_cols, live_blocks, send_rows, start, sketch):
    rows, slots, width, _ = blocks.shape
    rhs = start.shape[1]
    sk_rows = sketch.shape[0]
    directions, send_count = send_rows.shape[1:]
    chunk = rhs // ngy
    part = rhs // CHUNKS
    lanes = 2 * sk_rows
    count = STEPS + 1
    places = rows + directions * send_count + 1
    hbm = pl.BlockSpec(memory_space=pltpu.HBM)
    vmem = pl.BlockSpec(memory_space=pltpu.VMEM)
    dma = pltpu.SemaphoreType.DMA
    vectors, facs = pl.pallas_call(
        functools.partial(power_kernel, ngx, ngy),
        name="power",
        out_shape=[
            jax.ShapeDtypeStruct((count, rows, rhs, width), F32),
            jax.ShapeDtypeStruct((rhs, lanes), F32),
        ],
        in_specs=[hbm] * 6,
        out_specs=[vmem, vmem],
        scratch_shapes=[
            pltpu.SMEM(block_cols.shape, jnp.int32),
            pltpu.SMEM(live_blocks.shape, jnp.int32),
            pltpu.SMEM(send_rows.shape[1:], jnp.int32),
            pltpu.VMEM((rows, slots * width, width), BF16),
            pltpu.VMEM((width // 128, sk_rows * rows, 128), F32),
            pltpu.VMEM((rows, width, lanes), BF16),
            pltpu.VMEM((rows, part, width), F32),
            pltpu.VMEM((STEPS, CHUNKS, directions, send_count, part, width), BF16),
            pltpu.VMEM((rhs, lanes), F32),
            pltpu.VMEM((ngy, chunk, lanes), F32),
            pltpu.VMEM((ngy - 1, chunk, lanes), F32),
            pltpu.VMEM((ngx, chunk, lanes), F32),
            pltpu.VMEM((ngy, 2, chunk, lanes), F32),
            pltpu.VMEM((rhs, lanes), F32),
            pltpu.VMEM((2, CHUNKS, ngy, part // 2, lanes), F32),
            pltpu.VMEM((2, CHUNKS, ngx, part // 2, lanes), F32),
            dma((3,)),
            dma((CHUNKS + width // 128,)),
            dma((rows,)),
            dma((STEPS, CHUNKS, directions)),
            dma((STEPS, CHUNKS, directions)),
            dma((ngy - 1,)),
            dma((ngy - 1,)),
            dma((ngx - 1,)),
            dma((ngx - 1,)),
            dma((ngy - 1,)),
            dma((ngy - 1,)),
            dma((2, CHUNKS, ngy - 1)),
            dma((2, CHUNKS, ngy - 1)),
            dma((2, CHUNKS, ngx - 1)),
            dma((2, CHUNKS, ngx - 1)),
            *[
                pltpu.VMEM((places, part, width), BF16)
                for half in range(STEPS * CHUNKS)
            ],
            *[pltpu.VMEM((rows, part, width), F32) for c in range(CHUNKS)],
            *[pltpu.VMEM((rows, part, width), BF16) for c in range(CHUNKS)],
        ],
        compiler_params=pltpu.CompilerParams(
            collective_id=0, has_side_effects=True, vmem_limit_bytes=40 * 1024 * 1024
        ),
    )(
        *(
            pltpu.with_memory_space_constraint(array, pltpu.HBM)
            for array in (
                block_cols,
                live_blocks,
                send_rows[0],
                blocks.reshape(rows, slots * width, width),
                start,
                sketch.reshape(sk_rows * rows, width),
            )
        )
    )
    basis, factor = pl.pallas_call(
        finish_kernel,
        name="finish",
        out_shape=[
            jax.ShapeDtypeStruct((count, rows, rhs, width), F32),
            jax.ShapeDtypeStruct((count, count, rhs), F32),
        ],
        in_specs=[vmem, vmem],
        out_specs=[hbm, hbm],
        scratch_shapes=[
            pltpu.VMEM((1, rows, rhs, width), F32),
            pltpu.VMEM((count, count, rhs), F32),
            dma((count + 1,)),
            dma((2,)),
        ],
        compiler_params=pltpu.CompilerParams(vmem_limit_bytes=16 * 1024 * 1024),
    )(vectors, facs)
    return basis, factor


def solution(mesh):
    in_specs = (
        P(("gx", "gy"), None, None, None),
        P(("gx", "gy"), None),
        P(("gx", "gy")),
        P(("gx", "gy"), None, None),
        P(("gx", "gy"), None, None),
        P(None, ("gx", "gy"), None),
    )
    out_specs = (P(None, ("gx", "gy"), None, None), P())
    return jax.shard_map(
        functools.partial(on_device, mesh.shape["gx"], mesh.shape["gy"]),
        mesh=mesh,
        in_specs=in_specs,
        out_specs=out_specs,
        check_vma=False,
    )
```

```python
import functools

import jax
import jax.numpy as jnp
from jax import lax
from jax.experimental import pallas as pl
from jax.experimental.pallas import tpu as pltpu
from jax.sharding import PartitionSpec as P

STEPS = 3
CHUNKS = 2
MESH = pl.DeviceIdType.MESH
F32 = jnp.float32
BF16 = jnp.bfloat16


def split_bf16(x):
    high = x.astype(BF16)
    low = (x - high.astype(F32)).astype(BF16)
    return high, low


def combine(vectors, results, facs, first, past, begin, end, start=None):
    count, rows, rhs, width = vectors.shape
    group = 8
    base = count - results.shape[0]

    def body(n, carry):
        at = pl.ds(pl.multiple_of(n * group, group), group)
        f = facs[at, :]

        def spread(column):
            return jnp.broadcast_to(column, (group, width))

        upper = {
            (m, s): spread(f[:, m * count + s : m * count + s + 1])
            for s in range(first, past)
            for m in range(s)
        }
        inverse = {
            s: spread(1.0 / f[:, s * count + s : s * count + s + 1])
            for s in range(first, past)
        }
        for i in range(rows):
            done = [vectors[m, i, at, :] for m in range(first)]
            for s in range(first, past):
                if s == 0:
                    value = start[i, pl.ds(pl.multiple_of(n * group - begin, group), group), :]
                else:
                    value = vectors[s, i, at, :]
                for m in range(s):
                    value = value - upper[m, s] * done[m]
                value = value * inverse[s]
                done.append(value)
                results[s - base, i, at, :] = value
        return carry

    lax.fori_loop(begin // group, end // group, body, 0)


def power_kernel(
    ngx,
    ngy,
    cols_hbm,
    live_hbm,
    lists_hbm,
    blocks_hbm,
    start_hbm,
    sketch_hbm,
    basis,
    facs,
    cols,
    live,
    lists,
    blk,
    sk,
    shl,
    ahead,
    outgoing,
    kept,
    wsend,
    wrecv,
    gxbuf,
    qbuf,
    qfull,
    plane,
    summed,
    sem_lists,
    sem_local,
    sem_blk,
    halo_s,
    halo_r,
    p1s,
    p1r,
    p2s,
    p2r,
    p3s,
    p3r,
    t1s,
    t1r,
    t2s,
    t2r,
    *halves,
):
    ext = [halves[s * CHUNKS : (s + 1) * CHUNKS] for s in range(STEPS)]
    first = halves[STEPS * CHUNKS : (STEPS + 1) * CHUNKS]
    own = halves[(STEPS + 1) * CHUNKS :]
    count, rows, rhs, width = basis.shape
    part = rhs // CHUNKS
    slots = cols.shape[1]
    send_count = lists.shape[1]
    sk_rows = shl.shape[2] // 2
    lanes = 2 * sk_rows
    zero_slot = halves[0].shape[0] - 1
    chunk = rhs // ngy
    g, h = lax.axis_index("gx"), lax.axis_index("gy")

    barrier = pltpu.get_barrier_semaphore()
    for delta in range(1, ngx):
        pl.semaphore_signal(
            barrier, inc=1, device_id={"gx": lax.rem(g + delta, ngx)}, device_id_type=MESH
        )
    for delta in range(1, ngy):
        pl.semaphore_signal(
            barrier, inc=1, device_id={"gy": lax.rem(h + delta, ngy)}, device_id_type=MESH
        )

    def start_copy(c):
        rows_c = pl.ds(c * part, part)
        return pltpu.make_async_copy(
            start_hbm.at[:, rows_c], first[c], sem_local.at[c]
        )

    for c in range(CHUNKS):
        start_copy(c).start()
    scalar_loads = [
        pltpu.make_async_copy(source, target, sem_lists.at[n])
        for n, (source, target) in enumerate(
            ((lists_hbm, lists), (cols_hbm, cols), (live_hbm, live))
        )
    ]
    for load in scalar_loads:
        load.start()
    parts_wide = sk.shape[0]

    def sketch_copy(c):
        return pltpu.make_async_copy(
            sketch_hbm.at[:, pl.ds(c * 128, 128)], sk.at[c], sem_local.at[CHUNKS + c]
        )

    def block_copy(i):
        return pltpu.make_async_copy(blocks_hbm.at[i], blk.at[i], sem_blk.at[i])

    for half in halves[: STEPS * CHUNKS]:
        half[zero_slot] = jnp.zeros((part, width), BF16)

    far = jnp.where(g == ngx - 1, 2, 3)
    order = (far, 5 - far, 0, 1)

    def halo_copy(s, c, d):
        if isinstance(d, int) and d < 2:
            target = {"gy": lax.rem(h + (1 if d == 0 else ngy - 1), ngy)}
        else:
            target = {"gx": lax.rem(g + jnp.where(d == 2, 1, ngx - 1), ngx)}
        return pltpu.make_async_remote_copy(
            src_ref=outgoing.at[s, c, d],
            dst_ref=ext[s][c].at[pl.ds(rows + d * send_count, send_count)],
            send_sem=halo_s.at[s, c, d],
            recv_sem=halo_r.at[s, c, d],
            device_id=target,
            device_id_type=MESH,
        )

    def span(c):
        return slice(c * part, (c + 1) * part)

    def gather_outgoing(s, c, d):
        for j in range(send_count):
            outgoing[s, c, d, j] = own[c][lists[d, j]]

    def p1_copy(delta):
        to = lax.rem(h + delta, ngy)
        return pltpu.make_async_remote_copy(
            src_ref=wsend.at[to],
            dst_ref=wrecv.at[delta - 1],
            send_sem=p1s.at[delta - 1],
            recv_sem=p1r.at[delta - 1],
            device_id={"gy": to},
            device_id_type=MESH,
        )

    def p2_copy(delta):
        return pltpu.make_async_remote_copy(
            src_ref=gxbuf.at[g],
            dst_ref=gxbuf.at[g],
            send_sem=p2s.at[delta - 1],
            recv_sem=p2r.at[delta - 1],
            device_id={"gx": lax.rem(g + delta, ngx)},
            device_id_type=MESH,
        )

    def p3_copy(delta):
        return pltpu.make_async_remote_copy(
            src_ref=qbuf.at[h],
            dst_ref=qbuf.at[h],
            send_sem=p3s.at[delta - 1],
            recv_sem=p3r.at[delta - 1],
            device_id={"gy": lax.rem(h + delta, ngy)},
            device_id_type=MESH,
        )

    def t1_copy(n, c, delta):
        return pltpu.make_async_remote_copy(
            src_ref=plane.at[n, c, h],
            dst_ref=plane.at[n, c, h],
            send_sem=t1s.at[n, c, delta - 1],
            recv_sem=t1r.at[n, c, delta - 1],
            device_id={"gy": lax.rem(h + delta, ngy)},
            device_id_type=MESH,
        )

    def t2_copy(n, c, delta):
        return pltpu.make_async_remote_copy(
            src_ref=summed.at[n, c, g],
            dst_ref=summed.at[n, c, g],
            send_sem=t2s.at[n, c, delta - 1],
            recv_sem=t2r.at[n, c, delta - 1],
            device_id={"gx": lax.rem(g + delta, ngx)},
            device_id_type=MESH,
        )

    def low_half(n):
        return lax.broadcasted_iota(jnp.int32, (n, lanes), 1) < sk_rows

    def sketch_of(s, c):
        total = jnp.zeros((2 * part, lanes), F32)
        for i in range(rows):
            high, low = split_bf16(first[c][i] if s == 0 else basis[s, i, span(c), :])
            total = total + jnp.dot(
                jnp.concatenate([high, low], axis=0),
                shl[i],
                preferred_element_type=F32,
            )
        total = total[:part] + total[part:]
        return total + pltpu.roll(total, sk_rows, 1)

    def send_group(c, both):
        for k in range(part // chunk):
            wsend[c * (part // chunk) + k] = both[k * chunk : (k + 1) * chunk]
        if c == CHUNKS - 1:
            for delta in range(1, ngy):
                p1_copy(delta).start()

    def after_step(s, c):
        both = sketch_of(s, c)
        if s == 0:
            kept[span(c), :] = both
        elif s == 1:
            send_group(c, jnp.where(low_half(part), kept[span(c), :], both))
        else:
            half = part // 2
            plane[s - 2, c, h] = jnp.where(low_half(half), both[:half], both[half:])
            for delta in range(1, ngy):
                t1_copy(s - 2, c, delta).start()

    def finish_gy():
        total = wsend[h]
        for delta in range(1, ngy):
            p1_copy(delta).wait_recv()
            total = total + wrecv[delta - 1]
        gxbuf[g] = total
        for delta in range(1, ngx):
            p2_copy(delta).start()

    def orthogonal(w, earlier):
        residue = w
        found = []
        for unit in earlier:
            coefficient = jnp.sum(unit * w, axis=1, keepdims=True)
            found.append(coefficient)
            residue = residue - coefficient * unit
        square = jnp.sum(residue * residue, axis=1, keepdims=True)
        found.append(jnp.sqrt(square + 1e-06))
        return residue, found

    def put(f, s, found):
        lane = lax.broadcasted_iota(jnp.int32, f.shape, 1)
        for m, value in enumerate(found):
            f = jnp.where(lane == m * count + s, value, f)
        return f

    def finish_gx():
        for delta in range(1, ngx):
            p2_copy(delta).wait_recv()
        total = gxbuf[0]
        for other in range(1, ngx):
            total = total + gxbuf[other]
        units = []
        f = jnp.zeros((chunk, lanes), F32)
        for s in range(2):
            w = total[:, s * sk_rows : (s + 1) * sk_rows]
            residue, found = orthogonal(w, units)
            f = put(f, s, found)
            units.append(residue / found[-1])
        qbuf[h, 0] = jnp.concatenate(units, axis=1)
        qbuf[h, 1] = f
        for delta in range(1, ngy):
            p3_copy(delta).start()

    def take_units():
        for delta in range(1, ngy):
            p3_copy(delta).wait_recv()
        for k in range(ngy):
            qfull[k * chunk : (k + 1) * chunk, :] = qbuf[k, 0]
            facs[k * chunk : (k + 1) * chunk, :] = qbuf[k, 1]

    def sum_plane(n, c):
        for delta in range(1, ngy):
            t1_copy(n, c, delta).wait_recv()
        total = plane[n, c, 0]
        for other in range(1, ngy):
            total = total + plane[n, c, other]
        summed[n, c, g] = total

    def send_plane(n, c):
        for delta in range(1, ngx):
            t2_copy(n, c, delta).start()

    third = {}

    def finish_late(n, c):
        for delta in range(1, ngx):
            t2_copy(n, c, delta).wait_recv()
        total = summed[n, c, 0]
        for other in range(1, ngx):
            total = total + summed[n, c, other]
        w = jnp.concatenate([total[:, :sk_rows], total[:, sk_rows:]], axis=0)
        pair = qfull[span(c), :]
        earlier = [pair[:, :sk_rows], pair[:, sk_rows:]]
        if n == 1:
            earlier.append(third[c])
        residue, found = orthogonal(w, earlier)
        facs[span(c), :] = put(facs[span(c), :], n + 2, found)
        if n == 0:
            third[c] = residue / found[-1]

    for load in scalar_loads:
        load.wait()
    def prepare_sketch():
        for n in range(parts_wide):
            sketch_copy(n).wait()
            for i in range(rows):
                piece = sk[n, pl.ds(i, sk_rows, stride=rows), :]
                high, low = split_bf16(jnp.concatenate([piece, piece], axis=0).T)
                shl[i, n * 128 : (n + 1) * 128, :] = jnp.where(low_half(128), high, low)

    for c in range(CHUNKS):
        start_copy(c).wait()
        for i in range(rows):
            rounded = first[c][i].astype(BF16)
            own[c][i] = rounded
            ext[0][c][i] = rounded
        if c == 0:
            for n in range(parts_wide):
                sketch_copy(n).start()
            for i in range(rows):
                block_copy(i).start()
        for d in order:
            gather_outgoing(0, c, d)
        if c == 0:
            pl.semaphore_wait(barrier, ngx + ngy - 2)
        if c == 1:
            prepare_sketch()
        for n, d in enumerate(order):
            if c > 0 and n < 2:
                halo_copy(0, c - 1, d).wait_send()
            halo_copy(0, c, d).start()

    for c in range(CHUNKS):
        after_step(0, c)

    for s in range(STEPS):
        for c in range(CHUNKS):
            for i in range(rows):
                if s == 0 and c == 0:
                    block_copy(i).wait()
                ahead[i] = jnp.dot(own[c][i], blk[i, :width], preferred_element_type=F32)
            for d in order:
                halo_copy(s, c, d).wait_recv()

            def row(i):
                parts = []
                for k in range(1, slots):
                    index = jnp.where(k < live[i], cols[i, k], zero_slot)
                    parts.append(ext[s][c][index])
                picked = jnp.concatenate(parts, axis=1)
                for n in range(width // 128):
                    wide = slice(n * 128, (n + 1) * 128)
                    product = jnp.dot(
                        picked, blk[i, width:, wide], preferred_element_type=F32
                    )
                    product = product + ahead[i, :, wide]
                    basis[s + 1, i, span(c), wide] = product
                    if s + 1 < STEPS:
                        rounded = product.astype(BF16)
                        own[c][i, :, wide] = rounded
                        ext[s + 1][c][i, :, wide] = rounded

            for i in range(rows):
                row(i)
            if s + 1 < STEPS:
                for d in order:
                    gather_outgoing(s + 1, c, d)
                    halo_copy(s + 1, c, d).start()
            after_step(s + 1, c)
            if c == 1 and s == 1:
                finish_gy()

    finish_gx()
    for c in range(CHUNKS):
        sum_plane(0, c)
        send_plane(0, c)
    for c in range(CHUNKS):
        sum_plane(1, c)
        send_plane(1, c)
    take_units()
    for c in range(CHUNKS):
        finish_late(0, c)
        combine(basis, basis, facs, 0, STEPS, c * part, (c + 1) * part, first[c])
    for s in range(STEPS):
        for c in range(CHUNKS):
            for n, d in enumerate(order):
                if s > 0 or c == CHUNKS - 1 or n >= 2:
                    halo_copy(s, c, d).wait_send()
    for delta in range(1, ngy):
        p1_copy(delta).wait_send()
        p3_copy(delta).wait_send()
        for n in range(2):
            for c in range(CHUNKS):
                t1_copy(n, c, delta).wait_send()
    for delta in range(1, ngx):
        p2_copy(delta).wait_send()
        for c in range(CHUNKS):
            t2_copy(0, c, delta).wait_send()
    for c in range(CHUNKS):
        finish_late(1, c)
        if c + 1 < CHUNKS:
            combine(
                basis, basis, facs, STEPS, STEPS + 1, c * part, (c + 1) * part
            )

    for c in range(CHUNKS):
        for delta in range(1, ngx):
            t2_copy(1, c, delta).wait_send()


def finish_kernel(vectors, facs, basis_hbm, factor_hbm, last, turned, sem, sem_last):
    count, rows, rhs, width = vectors.shape
    pieces = sem_last.shape[0]
    begin = rhs - rhs // CHUNKS
    piece = (rhs - begin) // pieces

    def early_copy(s):
        at = pl.ds(0, begin if s == STEPS else rhs)
        return pltpu.make_async_copy(
            vectors.at[s, :, at], basis_hbm.at[s, :, at], sem.at[s]
        )

    def last_copy(n):
        at = pl.ds(begin + n * piece, piece)
        return pltpu.make_async_copy(
            last.at[0, :, at], basis_hbm.at[STEPS, :, at], sem_last.at[n]
        )

    factor_copy = pltpu.make_async_copy(turned, factor_hbm, sem.at[count])
    for s in range(count):
        early_copy(s).start()
    for n in range(pieces):
        at = begin + n * piece
        combine(vectors, last, facs, STEPS, STEPS + 1, at, at + piece)
        last_copy(n).start()
    lanes = facs[...].T
    for m in range(count):
        turned[m] = lanes[m * count : (m + 1) * count, :]
    factor_copy.start()
    for s in range(count):
        early_copy(s).wait()
    for n in range(pieces):
        last_copy(n).wait()
    factor_copy.wait()


def on_device(ngx, ngy, blocks, block_cols, live_blocks, send_rows, start, sketch):
    rows, slots, width, _ = blocks.shape
    rhs = start.shape[1]
    sk_rows = sketch.shape[0]
    directions, send_count = send_rows.shape[1:]
    chunk = rhs // ngy
    part = rhs // CHUNKS
    lanes = 2 * sk_rows
    count = STEPS + 1
    places = rows + directions * send_count + 1
    hbm = pl.BlockSpec(memory_space=pltpu.HBM)
    vmem = pl.BlockSpec(memory_space=pltpu.VMEM)
    dma = pltpu.SemaphoreType.DMA
    vectors, facs = pl.pallas_call(
        functools.partial(power_kernel, ngx, ngy),
        name="power",
        out_shape=[
            jax.ShapeDtypeStruct((count, rows, rhs, width), F32),
            jax.ShapeDtypeStruct((rhs, lanes), F32),
        ],
        in_specs=[hbm] * 6,
        out_specs=[vmem, vmem],
        scratch_shapes=[
            pltpu.SMEM(block_cols.shape, jnp.int32),
            pltpu.SMEM(live_blocks.shape, jnp.int32),
            pltpu.SMEM(send_rows.shape[1:], jnp.int32),
            pltpu.VMEM((rows, slots * width, width), BF16),
            pltpu.VMEM((width // 128, sk_rows * rows, 128), F32),
            pltpu.VMEM((rows, width, lanes), BF16),
            pltpu.VMEM((rows, part, width), F32),
            pltpu.VMEM((STEPS, CHUNKS, directions, send_count, part, width), BF16),
            pltpu.VMEM((rhs, lanes), F32),
            pltpu.VMEM((ngy, chunk, lanes), F32),
            pltpu.VMEM((ngy - 1, chunk, lanes), F32),
            pltpu.VMEM((ngx, chunk, lanes), F32),
            pltpu.VMEM((ngy, 2, chunk, lanes), F32),
            pltpu.VMEM((rhs, lanes), F32),
            pltpu.VMEM((2, CHUNKS, ngy, part // 2, lanes), F32),
            pltpu.VMEM((2, CHUNKS, ngx, part // 2, lanes), F32),
            dma((3,)),
            dma((CHUNKS + width // 128,)),
            dma((rows,)),
            dma((STEPS, CHUNKS, directions)),
            dma((STEPS, CHUNKS, directions)),
            dma((ngy - 1,)),
            dma((ngy - 1,)),
            dma((ngx - 1,)),
            dma((ngx - 1,)),
            dma((ngy - 1,)),
            dma((ngy - 1,)),
            dma((2, CHUNKS, ngy - 1)),
            dma((2, CHUNKS, ngy - 1)),
            dma((2, CHUNKS, ngx - 1)),
            dma((2, CHUNKS, ngx - 1)),
            *[
                pltpu.VMEM((places, part, width), BF16)
                for half in range(STEPS * CHUNKS)
            ],
            *[pltpu.VMEM((rows, part, width), F32) for c in range(CHUNKS)],
            *[pltpu.VMEM((rows, part, width), BF16) for c in range(CHUNKS)],
        ],
        compiler_params=pltpu.CompilerParams(
            collective_id=0, has_side_effects=True, vmem_limit_bytes=40 * 1024 * 1024
        ),
    )(
        *(
            pltpu.with_memory_space_constraint(array, pltpu.HBM)
            for array in (
                block_cols,
                live_blocks,
                send_rows[0],
                blocks.reshape(rows, slots * width, width),
                start,
                sketch.reshape(sk_rows * rows, width),
            )
        )
    )
    basis, factor = pl.pallas_call(
        finish_kernel,
        name="finish",
        out_shape=[
            jax.ShapeDtypeStruct((count, rows, rhs, width), F32),
            jax.ShapeDtypeStruct((count, count, rhs), F32),
        ],
        in_specs=[vmem, vmem],
        out_specs=[hbm, hbm],
        scratch_shapes=[
            pltpu.VMEM((1, rows, rhs, width), F32),
            pltpu.VMEM((count, count, rhs), F32),
            dma((count + 1,)),
            dma((1,)),
        ],
        compiler_params=pltpu.CompilerParams(vmem_limit_bytes=16 * 1024 * 1024),
    )(vectors, facs)
    return basis, factor


def solution(mesh):
    in_specs = (
        P(("gx", "gy"), None, None, None),
        P(("gx", "gy"), None),
        P(("gx", "gy")),
        P(("gx", "gy"), None, None),
        P(("gx", "gy"), None, None),
        P(None, ("gx", "gy"), None),
    )
    out_specs = (P(None, ("gx", "gy"), None, None), P())
    return jax.shard_map(
        functools.partial(on_device, mesh.shape["gx"], mesh.shape["gy"]),
        mesh=mesh,
        in_specs=in_specs,
        out_specs=out_specs,
        check_vma=False,
    )
```

```python
import functools

import jax
import jax.numpy as jnp
from jax import lax
from jax.experimental import pallas as pl
from jax.experimental.pallas import tpu as pltpu
from jax.sharding import PartitionSpec as P

STEPS = 3
CHUNKS = 2
MESH = pl.DeviceIdType.MESH
F32 = jnp.float32
BF16 = jnp.bfloat16


def split_bf16(x):
    high = x.astype(BF16)
    low = (x - high.astype(F32)).astype(BF16)
    return high, low


def combine(vectors, results, facs, first, past, begin, end, start=None):
    count, rows, rhs, width = vectors.shape
    group = 8
    base = count - results.shape[0]

    def body(n, carry):
        at = pl.ds(pl.multiple_of(n * group, group), group)
        f = facs[at, :]

        def spread(column):
            return jnp.broadcast_to(column, (group, width))

        upper = {
            (m, s): spread(f[:, m * count + s : m * count + s + 1])
            for s in range(first, past)
            for m in range(s)
        }
        inverse = {
            s: spread(1.0 / f[:, s * count + s : s * count + s + 1])
            for s in range(first, past)
        }
        for i in range(rows):
            done = [vectors[m, i, at, :] for m in range(first)]
            for s in range(first, past):
                if s == 0:
                    value = start[i, pl.ds(pl.multiple_of(n * group - begin, group), group), :]
                else:
                    value = vectors[s, i, at, :]
                for m in range(s):
                    value = value - upper[m, s] * done[m]
                value = value * inverse[s]
                done.append(value)
                results[s - base, i, at, :] = value
        return carry

    lax.fori_loop(begin // group, end // group, body, 0)


def power_kernel(
    ngx,
    ngy,
    cols_hbm,
    live_hbm,
    lists_hbm,
    blocks_hbm,
    start_hbm,
    sketch_hbm,
    basis,
    facs,
    cols,
    live,
    lists,
    blk,
    sk,
    shl,
    ahead,
    outgoing,
    kept,
    wsend,
    wrecv,
    gxbuf,
    qbuf,
    qfull,
    plane,
    summed,
    sem_lists,
    sem_local,
    sem_blk,
    halo_s,
    halo_r,
    p1s,
    p1r,
    p2s,
    p2r,
    p3s,
    p3r,
    t1s,
    t1r,
    t2s,
    t2r,
    *halves,
):
    ext = [halves[s * CHUNKS : (s + 1) * CHUNKS] for s in range(STEPS)]
    first = halves[STEPS * CHUNKS : (STEPS + 1) * CHUNKS]
    own = halves[(STEPS + 1) * CHUNKS :]
    count, rows, rhs, width = basis.shape
    part = rhs // CHUNKS
    slots = cols.shape[1]
    send_count = lists.shape[1]
    sk_rows = shl.shape[2] // 2
    lanes = 2 * sk_rows
    zero_slot = halves[0].shape[0] - 1
    chunk = rhs // ngy
    g, h = lax.axis_index("gx"), lax.axis_index("gy")

    barrier = pltpu.get_barrier_semaphore()
    for delta in range(1, ngx):
        pl.semaphore_signal(
            barrier, inc=1, device_id={"gx": lax.rem(g + delta, ngx)}, device_id_type=MESH
        )
    for delta in range(1, ngy):
        pl.semaphore_signal(
            barrier, inc=1, device_id={"gy": lax.rem(h + delta, ngy)}, device_id_type=MESH
        )

    def start_copy(c):
        rows_c = pl.ds(c * part, part)
        return pltpu.make_async_copy(
            start_hbm.at[:, rows_c], first[c], sem_local.at[c]
        )

    for c in range(CHUNKS):
        start_copy(c).start()
    scalar_loads = [
        pltpu.make_async_copy(source, target, sem_lists.at[n])
        for n, (source, target) in enumerate(
            ((lists_hbm, lists), (cols_hbm, cols), (live_hbm, live))
        )
    ]
    for load in scalar_loads:
        load.start()
    parts_wide = sk.shape[0]

    def sketch_copy(c):
        return pltpu.make_async_copy(
            sketch_hbm.at[:, pl.ds(c * 128, 128)], sk.at[c], sem_local.at[CHUNKS + c]
        )

    def block_copy(i):
        return pltpu.make_async_copy(blocks_hbm.at[i], blk.at[i], sem_blk.at[i])

    for half in halves[: STEPS * CHUNKS]:
        half[zero_slot] = jnp.zeros((part, width), BF16)

    far = jnp.where(g == ngx - 1, 2, 3)
    order = (far, 5 - far, 0, 1)

    def halo_copy(s, c, d):
        if isinstance(d, int) and d < 2:
            target = {"gy": lax.rem(h + (1 if d == 0 else ngy - 1), ngy)}
        else:
            target = {"gx": lax.rem(g + jnp.where(d == 2, 1, ngx - 1), ngx)}
        return pltpu.make_async_remote_copy(
            src_ref=outgoing.at[s, c, d],
            dst_ref=ext[s][c].at[pl.ds(rows + d * send_count, send_count)],
            send_sem=halo_s.at[s, c, d],
            recv_sem=halo_r.at[s, c, d],
            device_id=target,
            device_id_type=MESH,
        )

    def span(c):
        return slice(c * part, (c + 1) * part)

    def gather_outgoing(s, c, d):
        for j in range(send_count):
            outgoing[s, c, d, j] = own[c][lists[d, j]]

    def p1_copy(delta):
        to = lax.rem(h + delta, ngy)
        return pltpu.make_async_remote_copy(
            src_ref=wsend.at[to],
            dst_ref=wrecv.at[delta - 1],
            send_sem=p1s.at[delta - 1],
            recv_sem=p1r.at[delta - 1],
            device_id={"gy": to},
            device_id_type=MESH,
        )

    def p2_copy(delta):
        return pltpu.make_async_remote_copy(
            src_ref=gxbuf.at[g],
            dst_ref=gxbuf.at[g],
            send_sem=p2s.at[delta - 1],
            recv_sem=p2r.at[delta - 1],
            device_id={"gx": lax.rem(g + delta, ngx)},
            device_id_type=MESH,
        )

    def p3_copy(delta):
        return pltpu.make_async_remote_copy(
            src_ref=qbuf.at[h],
            dst_ref=qbuf.at[h],
            send_sem=p3s.at[delta - 1],
            recv_sem=p3r.at[delta - 1],
            device_id={"gy": lax.rem(h + delta, ngy)},
            device_id_type=MESH,
        )

    def t1_copy(n, c, delta):
        return pltpu.make_async_remote_copy(
            src_ref=plane.at[n, c, h],
            dst_ref=plane.at[n, c, h],
            send_sem=t1s.at[n, c, delta - 1],
            recv_sem=t1r.at[n, c, delta - 1],
            device_id={"gy": lax.rem(h + delta, ngy)},
            device_id_type=MESH,
        )

    def t2_copy(n, c, delta):
        return pltpu.make_async_remote_copy(
            src_ref=summed.at[n, c, g],
            dst_ref=summed.at[n, c, g],
            send_sem=t2s.at[n, c, delta - 1],
            recv_sem=t2r.at[n, c, delta - 1],
            device_id={"gx": lax.rem(g + delta, ngx)},
            device_id_type=MESH,
        )

    def low_half(n):
        return lax.broadcasted_iota(jnp.int32, (n, lanes), 1) < sk_rows

    def sketch_of(s, c):
        total = jnp.zeros((2 * part, lanes), F32)
        for i in range(rows):
            high, low = split_bf16(first[c][i] if s == 0 else basis[s, i, span(c), :])
            total = total + jnp.dot(
                jnp.concatenate([high, low], axis=0),
                shl[i],
                preferred_element_type=F32,
            )
        total = total[:part] + total[part:]
        return total + pltpu.roll(total, sk_rows, 1)

    def send_group(c, both):
        for k in range(part // chunk):
            wsend[c * (part // chunk) + k] = both[k * chunk : (k + 1) * chunk]
        if c == CHUNKS - 1:
            for delta in range(1, ngy):
                p1_copy(delta).start()

    def after_step(s, c):
        both = sketch_of(s, c)
        if s == 0:
            kept[span(c), :] = both
        elif s == 1:
            send_group(c, jnp.where(low_half(part), kept[span(c), :], both))
        else:
            half = part // 2
            plane[s - 2, c, h] = jnp.where(low_half(half), both[:half], both[half:])
            for delta in range(1, ngy):
                t1_copy(s - 2, c, delta).start()

    def finish_gy():
        total = wsend[h]
        for delta in range(1, ngy):
            p1_copy(delta).wait_recv()
            total = total + wrecv[delta - 1]
        gxbuf[g] = total
        for delta in range(1, ngx):
            p2_copy(delta).start()

    def orthogonal(w, earlier):
        residue = w
        found = []
        for unit in earlier:
            coefficient = jnp.sum(unit * w, axis=1, keepdims=True)
            found.append(coefficient)
            residue = residue - coefficient * unit
        square = jnp.sum(residue * residue, axis=1, keepdims=True)
        found.append(jnp.sqrt(square + 1e-06))
        return residue, found

    def put(f, s, found):
        lane = lax.broadcasted_iota(jnp.int32, f.shape, 1)
        for m, value in enumerate(found):
            f = jnp.where(lane == m * count + s, value, f)
        return f

    def finish_gx():
        for delta in range(1, ngx):
            p2_copy(delta).wait_recv()
        total = gxbuf[0]
        for other in range(1, ngx):
            total = total + gxbuf[other]
        units = []
        f = jnp.zeros((chunk, lanes), F32)
        for s in range(2):
            w = total[:, s * sk_rows : (s + 1) * sk_rows]
            residue, found = orthogonal(w, units)
            f = put(f, s, found)
            units.append(residue / found[-1])
        qbuf[h, 0] = jnp.concatenate(units, axis=1)
        qbuf[h, 1] = f
        for delta in range(1, ngy):
            p3_copy(delta).start()

    def take_units():
        for delta in range(1, ngy):
            p3_copy(delta).wait_recv()
        for k in range(ngy):
            qfull[k * chunk : (k + 1) * chunk, :] = qbuf[k, 0]
            facs[k * chunk : (k + 1) * chunk, :] = qbuf[k, 1]

    def sum_plane(n, c):
        for delta in range(1, ngy):
            t1_copy(n, c, delta).wait_recv()
        total = plane[n, c, 0]
        for other in range(1, ngy):
            total = total + plane[n, c, other]
        summed[n, c, g] = total

    def send_plane(n, c):
        for delta in range(1, ngx):
            t2_copy(n, c, delta).start()

    third = {}

    def finish_late(n, c):
        for delta in range(1, ngx):
            t2_copy(n, c, delta).wait_recv()
        total = summed[n, c, 0]
        for other in range(1, ngx):
            total = total + summed[n, c, other]
        w = jnp.concatenate([total[:, :sk_rows], total[:, sk_rows:]], axis=0)
        pair = qfull[span(c), :]
        earlier = [pair[:, :sk_rows], pair[:, sk_rows:]]
        if n == 1:
            earlier.append(third[c])
        residue, found = orthogonal(w, earlier)
        facs[span(c), :] = put(facs[span(c), :], n + 2, found)
        if n == 0:
            third[c] = residue / found[-1]

    for load in scalar_loads:
        load.wait()
    def prepare_sketch():
        for n in range(parts_wide):
            sketch_copy(n).wait()
            for i in range(rows):
                piece = sk[n, pl.ds(i, sk_rows, stride=rows), :]
                high, low = split_bf16(jnp.concatenate([piece, piece], axis=0).T)
                shl[i, n * 128 : (n + 1) * 128, :] = jnp.where(low_half(128), high, low)

    for c in range(CHUNKS):
        start_copy(c).wait()
        for i in range(rows):
            rounded = first[c][i].astype(BF16)
            own[c][i] = rounded
            ext[0][c][i] = rounded
        if c == 0:
            for n in range(parts_wide):
                sketch_copy(n).start()
            for i in range(rows):
                block_copy(i).start()
        for d in order:
            gather_outgoing(0, c, d)
        if c == 0:
            pl.semaphore_wait(barrier, ngx + ngy - 2)
        if c == 1:
            prepare_sketch()
        for n, d in enumerate(order):
            if c > 0 and n < 2:
                halo_copy(0, c - 1, d).wait_send()
            halo_copy(0, c, d).start()

    for c in range(CHUNKS):
        after_step(0, c)

    for s in range(STEPS):
        for c in range(CHUNKS):
            for i in range(rows):
                if s == 0 and c == 0:
                    block_copy(i).wait()
                ahead[i] = jnp.dot(own[c][i], blk[i, :width], preferred_element_type=F32)
            for d in order:
                halo_copy(s, c, d).wait_recv()

            def row(i):
                parts = []
                for k in range(1, slots):
                    index = jnp.where(k < live[i], cols[i, k], zero_slot)
                    parts.append(ext[s][c][index])
                picked = jnp.concatenate(parts, axis=1)
                for n in range(width // 128):
                    wide = slice(n * 128, (n + 1) * 128)
                    product = jnp.dot(
                        picked, blk[i, width:, wide], preferred_element_type=F32
                    )
                    product = product + ahead[i, :, wide]
                    basis[s + 1, i, span(c), wide] = product
                    if s + 1 < STEPS:
                        rounded = product.astype(BF16)
                        own[c][i, :, wide] = rounded
                        ext[s + 1][c][i, :, wide] = rounded

            for i in range(rows):
                row(i)
            if s + 1 < STEPS:
                for d in order:
                    gather_outgoing(s + 1, c, d)
                    halo_copy(s + 1, c, d).start()
            after_step(s + 1, c)
            if c == 1 and s == 1:
                finish_gy()

    for c in range(CHUNKS):
        sum_plane(0, c)
        send_plane(0, c)
    finish_gx()
    for c in range(CHUNKS):
        sum_plane(1, c)
        send_plane(1, c)
    take_units()
    for c in range(CHUNKS):
        finish_late(0, c)
        combine(basis, basis, facs, 0, STEPS, c * part, (c + 1) * part, first[c])
    for s in range(STEPS):
        for c in range(CHUNKS):
            for n, d in enumerate(order):
                if s > 0 or c == CHUNKS - 1 or n >= 2:
                    halo_copy(s, c, d).wait_send()
    for delta in range(1, ngy):
        p1_copy(delta).wait_send()
        p3_copy(delta).wait_send()
        for n in range(2):
            for c in range(CHUNKS):
                t1_copy(n, c, delta).wait_send()
    for delta in range(1, ngx):
        p2_copy(delta).wait_send()
        for c in range(CHUNKS):
            t2_copy(0, c, delta).wait_send()
    for c in range(CHUNKS):
        finish_late(1, c)
        if c + 1 < CHUNKS:
            combine(
                basis, basis, facs, STEPS, STEPS + 1, c * part, (c + 1) * part
            )
            for delta in range(1, ngx):
                t2_copy(1, c, delta).wait_send()

    for delta in range(1, ngx):
        t2_copy(1, CHUNKS - 1, delta).wait_send()


def finish_kernel(vectors, facs, basis_hbm, factor_hbm, last, turned, sem, sem_last):
    count, rows, rhs, width = vectors.shape
    pieces = sem_last.shape[0]
    begin = rhs - rhs // CHUNKS
    piece = (rhs - begin) // pieces

    def early_copy(s):
        at = pl.ds(0, begin if s == STEPS else rhs)
        return pltpu.make_async_copy(
            vectors.at[s, :, at], basis_hbm.at[s, :, at], sem.at[s]
        )

    def last_copy(n):
        at = pl.ds(begin + n * piece, piece)
        return pltpu.make_async_copy(
            last.at[0, :, at], basis_hbm.at[STEPS, :, at], sem_last.at[n]
        )

    factor_copy = pltpu.make_async_copy(turned, factor_hbm, sem.at[count])
    for s in range(count):
        early_copy(s).start()
    for n in range(pieces):
        at = begin + n * piece
        combine(vectors, last, facs, STEPS, STEPS + 1, at, at + piece)
        last_copy(n).start()
    lanes = facs[...].T
    for m in range(count):
        turned[m] = lanes[m * count : (m + 1) * count, :]
    factor_copy.start()
    for s in range(count):
        early_copy(s).wait()
    for n in range(pieces):
        last_copy(n).wait()
    factor_copy.wait()


def on_device(ngx, ngy, blocks, block_cols, live_blocks, send_rows, start, sketch):
    rows, slots, width, _ = blocks.shape
    rhs = start.shape[1]
    sk_rows = sketch.shape[0]
    directions, send_count = send_rows.shape[1:]
    chunk = rhs // ngy
    part = rhs // CHUNKS
    lanes = 2 * sk_rows
    count = STEPS + 1
    places = rows + directions * send_count + 1
    hbm = pl.BlockSpec(memory_space=pltpu.HBM)
    vmem = pl.BlockSpec(memory_space=pltpu.VMEM)
    dma = pltpu.SemaphoreType.DMA
    vectors, facs = pl.pallas_call(
        functools.partial(power_kernel, ngx, ngy),
        name="power",
        out_shape=[
            jax.ShapeDtypeStruct((count, rows, rhs, width), F32),
            jax.ShapeDtypeStruct((rhs, lanes), F32),
        ],
        in_specs=[hbm] * 6,
        out_specs=[vmem, vmem],
        scratch_shapes=[
            pltpu.SMEM(block_cols.shape, jnp.int32),
            pltpu.SMEM(live_blocks.shape, jnp.int32),
            pltpu.SMEM(send_rows.shape[1:], jnp.int32),
            pltpu.VMEM((rows, slots * width, width), BF16),
            pltpu.VMEM((width // 128, sk_rows * rows, 128), F32),
            pltpu.VMEM((rows, width, lanes), BF16),
            pltpu.VMEM((rows, part, width), F32),
            pltpu.VMEM((STEPS, CHUNKS, directions, send_count, part, width), BF16),
            pltpu.VMEM((rhs, lanes), F32),
            pltpu.VMEM((ngy, chunk, lanes), F32),
            pltpu.VMEM((ngy - 1, chunk, lanes), F32),
            pltpu.VMEM((ngx, chunk, lanes), F32),
            pltpu.VMEM((ngy, 2, chunk, lanes), F32),
            pltpu.VMEM((rhs, lanes), F32),
            pltpu.VMEM((2, CHUNKS, ngy, part // 2, lanes), F32),
            pltpu.VMEM((2, CHUNKS, ngx, part // 2, lanes), F32),
            dma((3,)),
            dma((CHUNKS + width // 128,)),
            dma((rows,)),
            dma((STEPS, CHUNKS, directions)),
            dma((STEPS, CHUNKS, directions)),
            dma((ngy - 1,)),
            dma((ngy - 1,)),
            dma((ngx - 1,)),
            dma((ngx - 1,)),
            dma((ngy - 1,)),
            dma((ngy - 1,)),
            dma((2, CHUNKS, ngy - 1)),
            dma((2, CHUNKS, ngy - 1)),
            dma((2, CHUNKS, ngx - 1)),
            dma((2, CHUNKS, ngx - 1)),
            *[
                pltpu.VMEM((places, part, width), BF16)
                for half in range(STEPS * CHUNKS)
            ],
            *[pltpu.VMEM((rows, part, width), F32) for c in range(CHUNKS)],
            *[pltpu.VMEM((rows, part, width), BF16) for c in range(CHUNKS)],
        ],
        compiler_params=pltpu.CompilerParams(
            collective_id=0, has_side_effects=True, vmem_limit_bytes=40 * 1024 * 1024
        ),
    )(
        *(
            pltpu.with_memory_space_constraint(array, pltpu.HBM)
            for array in (
                block_cols,
                live_blocks,
                send_rows[0],
                blocks.reshape(rows, slots * width, width),
                start,
                sketch.reshape(sk_rows * rows, width),
            )
        )
    )
    basis, factor = pl.pallas_call(
        finish_kernel,
        name="finish",
        out_shape=[
            jax.ShapeDtypeStruct((count, rows, rhs, width), F32),
            jax.ShapeDtypeStruct((count, count, rhs), F32),
        ],
        in_specs=[vmem, vmem],
        out_specs=[hbm, hbm],
        scratch_shapes=[
            pltpu.VMEM((1, rows, rhs, width), F32),
            pltpu.VMEM((count, count, rhs), F32),
            dma((count + 1,)),
            dma((1,)),
        ],
        compiler_params=pltpu.CompilerParams(vmem_limit_bytes=16 * 1024 * 1024),
    )(vectors, facs)
    return basis, factor


def solution(mesh):
    in_specs = (
        P(("gx", "gy"), None, None, None),
        P(("gx", "gy"), None),
        P(("gx", "gy")),
        P(("gx", "gy"), None, None),
        P(("gx", "gy"), None, None),
        P(None, ("gx", "gy"), None),
    )
    out_specs = (P(None, ("gx", "gy"), None, None), P())
    return jax.shard_map(
        functools.partial(on_device, mesh.shape["gx"], mesh.shape["gy"]),
        mesh=mesh,
        in_specs=in_specs,
        out_specs=out_specs,
        check_vma=False,
    )
```
